512 devices in a mesh: enc: 32 (over y, x), section: 8 (over z_lo, core), llmdp: 2 (over z_hi).
Axes of the slice: x: 4, y: 8, z: 8 (z_hi: 2, z_lo: 4; z = z_hi * 4 + z_lo), core: 2. Of those that a mesh axis runs over, the one named last changes fastest.
Arguments:
- patches: bfloat16 [8192, 3200], P('enc', ('section', 'llmdp')), may hold values from -6 to 6
- gain: float32 [3200], replicated, may hold values from 0.25 to 1.75
- shift: float32 [3200], replicated, may hold values from -3 to 3
- proj_weight: bfloat16 [3200, 8192], P('enc', ('section', 'llmdp')), may hold values from -0.109375 to 0.109375
- llm_rank: int32 [8192, 1], P('enc'), may hold values from 0 to 31; in each aligned block of 256 rows (0 to 255, 256 to 511, ...) at most 24 rows name the same one
- embed_grad: bfloat16 [24576, 8192], P('enc', ('section', 'llmdp')), may hold values from -0.59765625 to 0.59765625
Outputs:
- embeds_recv: bfloat16 [24576, 8192], P('enc', ('section', 'llmdp'))
- hidden_state_gradient: bfloat16 [8192, 3200], P('enc', ('section', 'llmdp'))
- grad_weight: float32 [3200, 8192], P('enc', ('section', 'llmdp'))
- gain_gradient: float32 [3200], P(('section', 'llmdp'))
- grad_shift: float32 [3200], P(('section', 'llmdp'))
The draws below stay inside these ranges and needn't reach their ends.
Inputs may be any that keep to these rules, and one draw needn't show every extreme that they name: `llm_rank`: among the 256 rows of one device, at most 24 name the same owner, a bound that some block reaches.
All inputs are finite; a program needn't handle non-finite values.
Results may differ from the reference program's by a relative error of at most 0.018.
Values may be sent and summed in bfloat16 or wider, within the bound.
No kernel may reach another device: no remote copies, remote signals or barrier semaphores. Data moves between devices by JAX's collectives and lax.ppermute only.
A program may use at most 64 MiB of HBM per device.

```python
import math
import jax
import jax.numpy as jnp
import numpy as np
from jax import lax

D = 3200
E = 8192
TOK_DEV = 256
TOKENS = 8192
MOST = 24
RECV = 24576
N_ENC = 32
N_SECTION = 8
N_LLMDP = 2


def level_of(own_key, shape, split, least, largest):
    factor_of = 1.0
    for axis_at, blocks in split:
        steps = jax.random.uniform(jax.random.fold_in(jax.random.fold_in(own_key, 6), axis_at), (blocks,), jnp.float32, least / len(split), largest / len(split))
        factor_of = factor_of * jnp.repeat(jnp.exp(steps), shape[axis_at] // blocks).reshape((-1,) + (1,) * (len(shape) - 1 - axis_at))
    return factor_of


def shared_out(stream_key, own, number, rows, count, top, limit, lean):
    order = jax.random.permutation(stream_key, count)
    heavy_load, common = portions_of(count, rows * top, limit, lean, True), portions_of(count, rows * top, limit, lean, False)
    places = jnp.arange(count)

    def named(sizes, turn):
        used = int((sizes > 0).sum())
        fixed = max(1, used // 4)
        moved = fixed + (places - fixed + turn * (used - fixed)) % max(1, count - fixed)
        return jnp.zeros((count,), jnp.int32).at[order[jnp.where(places < fixed, places, moved)]].set(jnp.asarray(sizes, jnp.int32))

    sizes = jnp.where(number % 4 == 0, named(heavy_load, number // 4), named(common, number - number // 4 - 1))
    mixed = jax.random.permutation(jax.random.fold_in(own, 3), count)
    source_of, receiver = mixed[0:count // 2 * 2:2], mixed[1:count // 2 * 2:2]
    slack = jnp.minimum(sizes[source_of] - 1, limit - sizes[receiver]) // 2
    slack = jnp.where((source_of == order[0]) | (receiver == order[0]) | (sizes[receiver] == 0), 0, jnp.maximum(slack, 0))
    moved = jax.random.randint(jax.random.fold_in(own, 4), (count // 2,), 0, 1 << 20) % (slack + 1)
    sizes = sizes.at[source_of].add(-moved).at[receiver].add(moved)
    labels = jnp.searchsorted(jnp.cumsum(sizes), jnp.arange(rows * top), side="right").astype(jnp.int32)
    listing = labels.reshape(top, rows).T
    listing = listing[jax.random.permutation(jax.random.fold_in(own, 1), rows)]
    turn = jax.random.randint(jax.random.fold_in(own, 2), (rows, 1), 0, top)
    return jnp.take_along_axis(listing, (jnp.arange(top)[None, :] + turn) % top, axis=1)


def portions_of(count, total, reach, slope, full):
    weights = [(1 << 20) // math.isqrt(grade ** slope) + 1 for grade in range(1, count + 1)]
    largest = reach if full else min(reach, max(-(-total // count), total * weights[0] // sum(weights)))
    least = 1 if total - largest >= count - 1 else 0
    counts, spare = [largest] + [least] * (count - 1), total - largest - least * (count - 1)
    while spare > 0:
        movable = [i for i in range(1, count) if counts[i] < largest] or [i for i in range(1, count) if counts[i] < reach]
        whole, remaining = sum([weights[i] for i in movable]), spare
        for i in movable:
            more = min(reach - counts[i], max(1, remaining * weights[i] // whole), spare)
            counts[i] = counts[i] + more
            spare = spare - more
    return np.array(counts)


def noise(own_key, extent, scale, most, pieces=(), held_as=jnp.bfloat16):
    factor_of = level_of(own_key, extent, pieces, -0.22, 0.18) if pieces else 1.0
    array = jax.random.normal(own_key, extent, jnp.float32) * scale * factor_of
    return jnp.minimum(jnp.maximum(array, -most), most).astype(held_as)


def setup_inputs(seed: int = 0) -> dict:
    arg_keys = jax.random.split(jax.random.key(seed), 7)
    patches = noise(arg_keys[0], (TOKENS, D), 1.0, 6.0, ((0, 32), (1, 16)))
    gain = jnp.clip(1.0 + 0.15 * jax.random.normal(arg_keys[1], (D,), jnp.float32), 0.25, 1.75)
    shift = noise(arg_keys[2], (D,), 0.5, 3.0, (), jnp.float32)
    proj_weight = noise(arg_keys[3], (D, E), D ** -0.5, 0.109375, ((0, 32), (1, 16)))
    llm_rank_keys = jax.random.split(jax.random.fold_in(arg_keys[4], 1), TOKENS // TOK_DEV)
    llm_rank_turns = jax.random.permutation(jax.random.fold_in(arg_keys[4], 3), TOKENS // TOK_DEV)
    llm_rank = jax.vmap(lambda own, number: shared_out(jax.random.fold_in(arg_keys[4], 2), own, number, TOK_DEV, N_ENC, 1, MOST, 2))(llm_rank_keys, llm_rank_turns).reshape((TOKENS, 1))
    embed_grad = noise(arg_keys[5], (RECV, E), 0.1, 0.59765625, ((0, 32), (1, 16)))
    return {"patches": patches, "gain": gain, "shift": shift, "proj_weight": proj_weight, "llm_rank": llm_rank, "embed_grad": embed_grad}


EPSILON = 1e-05

def reference(patches, gain, shift, proj_weight, llm_rank, embed_grad):
    value_entries = patches.astype(jnp.float32)
    row_average = lax.optimization_barrier(jnp.mean(value_entries, 1, keepdims=True))
    variance = lax.optimization_barrier(jnp.mean(value_entries * value_entries, 1, keepdims=True)) - row_average * row_average
    inverse_deviation = lax.rsqrt(variance + EPSILON)
    standardized_rows = (value_entries - row_average) * inverse_deviation
    normed_hidden = (standardized_rows * gain + shift).astype(jnp.bfloat16)
    embed = jnp.dot(normed_hidden, proj_weight, preferred_element_type=jnp.float32).astype(jnp.bfloat16)
    target = llm_rank[:, 0].astype(jnp.int32).reshape(N_ENC, TOK_DEV)
    owners = jnp.arange(N_ENC, dtype=jnp.int32)
    hits = (target[:, :, None] == owners[None, None, :]).astype(jnp.int32)
    rank = lax.optimization_barrier(jnp.sum((jnp.cumsum(hits, 1) - hits) * hits, 2)).astype(jnp.int32)
    slot = (target * (N_ENC * MOST) + owners[:, None] * MOST + rank).reshape(-1).astype(jnp.int32)
    embeds_recv = jnp.zeros((RECV, E), jnp.bfloat16).at[slot].set(embed)
    d_embed = embed_grad[slot]
    groups = N_SECTION * N_LLMDP
    group_cols = E // groups

    def group_step(total, index):
        start = (index * group_cols).astype(jnp.int32)
        grad_part = lax.dynamic_slice_in_dim(d_embed, start, group_cols, 1)
        weight_part = lax.dynamic_slice_in_dim(proj_weight, start, group_cols, 1)
        term = lax.dot_general(grad_part, weight_part, (((1,), (1,)), ((), ())), preferred_element_type=jnp.float32)
        return (total + lax.optimization_barrier(term.astype(jnp.bfloat16)).astype(jnp.float32), None)
    normalized_gradient, _ = lax.scan(group_step, jnp.zeros((TOKENS, D), jnp.float32), jnp.arange(groups, dtype=jnp.int32))

    def block_step(total, pair):
        term = lax.dot_general(pair[0], pair[1], (((0,), (0,)), ((), ())), preferred_element_type=jnp.float32)
        return (total + lax.optimization_barrier(term.astype(jnp.bfloat16)).astype(jnp.float32), None)
    grad_weight, _ = lax.scan(block_step, jnp.zeros((D, E), jnp.float32), (normed_hidden.reshape(N_ENC, TOK_DEV, D), d_embed.reshape(N_ENC, TOK_DEV, E)))
    centered_gradient = normalized_gradient * gain
    gradient_row_average = lax.optimization_barrier(jnp.mean(centered_gradient, 1, keepdims=True))
    gradient_cross_product = lax.optimization_barrier(jnp.mean(centered_gradient * standardized_rows, 1, keepdims=True))
    hidden_state_gradient = (inverse_deviation * (centered_gradient - gradient_row_average - standardized_rows * gradient_cross_product)).astype(jnp.bfloat16)
    gain_gradient = lax.optimization_barrier(jnp.sum(normalized_gradient * standardized_rows, 0))
    grad_shift = lax.optimization_barrier(jnp.sum(normalized_gradient, 0))
    return (embeds_recv, hidden_state_gradient, grad_weight, gain_gradient, grad_shift)
```

```python
import functools

import jax
import jax.numpy as jnp
from jax import lax
from jax.experimental import pallas as pl
from jax.experimental.pallas import tpu as pltpu
from jax.sharding import Mesh
from jax.sharding import PartitionSpec as P

ENC = ("y", "x")
COLS = ("zl", "co", "zh")
EPSILON = 1e-05
F32 = jnp.float32
BF16 = jnp.bfloat16
VMEM = pl.BlockSpec(memory_space=pltpu.VMEM)
SMEM = pl.BlockSpec(memory_space=pltpu.SMEM)
PARAMS = pltpu.CompilerParams(vmem_limit_bytes=48 * 1024 * 1024)
EXTRA = 8


def exchange(x, axes):
    return lax.all_to_all(x, axes, 0, 0, tiled=True)


def copies(x, axes):
    count = lax.axis_size(axes)
    return exchange(jnp.broadcast_to(x[None], (count, *x.shape)), axes)


def shifted(x, axes, step):
    count = lax.axis_size(axes)
    return lax.ppermute(x, axes, [(i, (i + step) % count) for i in range(count)])


def along_z(x, step):
    n_zl, n_zh = lax.axis_size("zl"), lax.axis_size("zh")
    count = n_zl * n_zh
    at = [(z % n_zl) * n_zh + z // n_zl for z in range(count)]
    return lax.ppermute(x, ("zl", "zh"), [(at[z], at[(z + step) % count]) for z in range(count)])


def core_swap(x):
    return lax.ppermute(x, "co", [(0, 1), (1, 0)])


def block_of(z, core, n_zl, n_zh):
    return (z % n_zl) * (2 * n_zh) + core * n_zh + z // n_zl


def norm_kernel(n_zl, n_zh, slots, place, mine, other, gain, shift, normed, normed_x, stats):
    n_z = n_zl * n_zh
    z, core = place[0], place[1]
    own_width, rows = mine.shape[1:]
    width = 2 * n_z * own_width
    half = own_width // slots
    n_x = normed_x.shape[0]

    def totals(k, carry):
        total, squares = carry
        for ref in (mine, other):
            x = ref[k].astype(F32)
            total = total + jnp.sum(x, 0, keepdims=True)
            squares = squares + jnp.sum(x * x, 0, keepdims=True)
        return total, squares

    zero = jnp.zeros((1, rows), F32)
    total, squares = lax.fori_loop(0, n_z, totals, (zero, zero))
    mean = total / width
    inv = lax.rsqrt(squares / width - mean * mean + EPSILON)
    stats[0:1, :] = mean
    stats[1:2, :] = inv
    normed_x[...] = jnp.zeros_like(normed_x)

    def apply(k, carry):
        source = lax.rem(z - k + n_z, n_z)
        for ref, owner in ((mine, core), (other, 1 - core)):
            b = block_of(source, owner, n_zl, n_zh)
            scale = jnp.concatenate([gain[b]] * (rows // 128), 1)
            offset = jnp.concatenate([shift[b]] * (rows // 128), 1)
            value = (ref[k].astype(F32) - mean) * inv * scale + offset
            normed[b] = value.astype(BF16)
            for part in range(slots):
                slot = b * slots + part
                piece = value[part * half : (part + 1) * half]
                normed_x[slot % n_x, slot // n_x, 0:half, :] = piece.astype(BF16)
        return carry

    lax.fori_loop(0, n_z, apply, 0)


def part_kernel(n_zl, n_zh, place, weight, d_embed, mine, other, gain, stats, keep, send):
    n_z = n_zl * n_zh
    z, core = place[0], place[1]
    own_width, rows = mine.shape[1:]
    mean, inv = stats[0:1, :], stats[1:2, :]

    def step(k, carry):
        plain, cross = carry
        target = lax.rem(z + k, n_z)
        back = lax.rem(n_z - k, n_z)
        for source, owner, out in ((mine, core, keep), (other, 1 - core, send)):
            b = block_of(target, owner, n_zl, n_zh)
            part = lax.dot_general(
                weight[b], d_embed[...], (((1,), (1,)), ((), ())), preferred_element_type=F32
            ).astype(BF16)
            out[k, 0:own_width, :] = part
            scale = jnp.concatenate([gain[b]] * (rows // 128), 1)
            scaled = part.astype(F32) * scale
            xhat = (source[back].astype(F32) - mean) * inv
            plain = plain + jnp.sum(scaled, 0, keepdims=True)
            cross = cross + jnp.sum(scaled * xhat, 0, keepdims=True)
        return plain, cross

    zero = jnp.zeros((1, rows), F32)
    plain, cross = lax.fori_loop(0, n_z, step, (zero, zero))
    high_plain, high_cross = plain.astype(BF16), cross.astype(BF16)
    tail = jnp.concatenate(
        [
            high_plain.astype(F32),
            plain - high_plain.astype(F32),
            high_cross.astype(F32),
            cross - high_cross.astype(F32),
            jnp.zeros((EXTRA - 4, rows), F32),
        ],
        0,
    ).astype(BF16)
    for k in range(n_z):
        keep[k, own_width:, :] = tail
        send[k, own_width:, :] = tail


def pair_kernel(keep, recv, *outs):
    own_width = keep.shape[1] - EXTRA
    rows = keep.shape[2]
    tail = keep[0, own_width:, :].astype(F32) + recv[0, own_width:, :].astype(F32)
    plain, cross = tail[0:1] + tail[1:2], tail[2:3] + tail[3:4]
    high_plain, high_cross = plain.astype(BF16).astype(F32), cross.astype(BF16).astype(F32)
    tail = jnp.concatenate(
        [
            high_plain,
            plain - high_plain,
            high_cross,
            cross - high_cross,
            jnp.zeros((EXTRA - 4, rows), F32),
        ],
        0,
    ).astype(BF16)
    for k, out in enumerate(outs):
        pair = keep[k, 0:own_width, :].astype(F32) + recv[k, 0:own_width, :].astype(F32)
        out[0:own_width, :] = pair.astype(BF16)
        out[own_width:, :] = tail


def body(patches, gain, shift, proj_weight, llm_rank, embed_grad):
    rows, own_width = patches.shape
    width = gain.shape[0]
    out_cols = proj_weight.shape[1]
    n_y, n_x = lax.axis_size("y"), lax.axis_size("x")
    n_zl, n_zh = lax.axis_size("zl"), lax.axis_size("zh")
    n_z = n_zl * n_zh
    senders = n_y * n_x
    slice_rows = proj_weight.shape[0]
    padded_rows = -(-slice_rows // 8) * 8
    slots = own_width // slice_rows
    most = embed_grad.shape[0] // senders
    blocks = width // own_width
    core, x_at = lax.axis_index("co"), lax.axis_index("x")
    place = jnp.stack([lax.axis_index("zh") * n_zl + lax.axis_index("zl"), core]).astype(jnp.int32)

    weight_rel = [proj_weight] + [shifted(proj_weight, "x", k) for k in range(1, n_x)]
    returned = exchange(embed_grad.reshape(senders, most, out_cols), ENC)
    ordered = jnp.stack([weight_rel[-i % n_x] for i in range(n_x)] * 2)
    weight_x = lax.dynamic_slice_in_dim(ordered, lax.rem(n_x - x_at, n_x), n_x, 0)
    weight = lax.all_gather(weight_x.reshape(n_x * slice_rows, out_cols), "y", axis=0, tiled=True)

    own_t = patches.T
    mine = jnp.stack([own_t] + [along_z(own_t, k) for k in range(1, n_z)])
    other = core_swap(mine)
    gain_wide = jnp.broadcast_to(gain.reshape(blocks, own_width, 1), (blocks, own_width, 128))
    shift_wide = jnp.broadcast_to(shift.reshape(blocks, own_width, 1), (blocks, own_width, 128))
    normed, normed_x, stats = pl.pallas_call(
        functools.partial(norm_kernel, n_zl, n_zh, slots),
        out_shape=(
            jax.ShapeDtypeStruct((blocks, own_width, rows), BF16),
            jax.ShapeDtypeStruct((n_x, n_y, padded_rows, rows), BF16),
            jax.ShapeDtypeStruct((8, rows), F32),
        ),
        in_specs=[SMEM] + [VMEM] * 4,
        out_specs=(VMEM,) * 3,
        compiler_params=PARAMS,
        name="norm",
    )(place, mine, other, gain_wide, shift_wide)
    mean, inv = stats[0], stats[1]

    target = llm_rank[:, 0]
    owners = jnp.arange(senders, dtype=jnp.int32)
    hits = (target[:, None] == owners[None, :]).astype(jnp.int32)
    rank = jnp.sum((jnp.cumsum(hits, 0) - hits) * hits, 1)
    slot = target * most + rank
    d_embed = returned.reshape(senders * most, out_cols)[slot]

    stack_x = normed_x.reshape(n_x, n_y * padded_rows, rows)

    def grad_block(step):
        lhs = lax.dynamic_index_in_dim(stack_x, lax.rem(x_at + step, n_x), 0, keepdims=False)
        return jnp.dot(lhs, d_embed, preferred_element_type=F32).astype(BF16)

    grad_x = sum(
        [shifted(grad_block(k), "x", k).astype(F32) for k in range(1, n_x)],
        grad_block(0).astype(F32),
    )
    embed = lax.dot_general(
        normed.reshape(width, rows), weight, (((0,), (0,)), ((), ())), preferred_element_type=F32
    ).astype(BF16)
    outgoing = jnp.zeros((senders * most, out_cols), BF16).at[slot].set(embed)
    embeds_recv = exchange(outgoing.reshape(senders, most, out_cols), ENC).reshape(
        senders * most, out_cols
    )

    grad_x, embeds_recv = lax.optimization_barrier((grad_x.astype(BF16), embeds_recv))
    grad_y = exchange(grad_x.reshape(n_y, padded_rows, out_cols), "y")
    grad_weight = jnp.sum(grad_y.astype(F32), 0)[:slice_rows]

    half_shape = jax.ShapeDtypeStruct((n_z, own_width + EXTRA, rows), BF16)
    keep, send = pl.pallas_call(
        functools.partial(part_kernel, n_zl, n_zh),
        out_shape=(half_shape, half_shape),
        in_specs=[SMEM] + [VMEM] * 6,
        out_specs=(VMEM,) * 2,
        compiler_params=PARAMS,
        name="part",
    )(place, weight.reshape(blocks, own_width, out_cols), d_embed, mine, other, gain_wide, stats)
    pairs = pl.pallas_call(
        pair_kernel,
        out_shape=(jax.ShapeDtypeStruct((own_width + EXTRA, rows), BF16),) * n_z,
        in_specs=[VMEM] * 2,
        out_specs=(VMEM,) * n_z,
        compiler_params=PARAMS,
        name="pair",
    )(keep, core_swap(send))
    columns = sum(
        [along_z(pairs[k], k).astype(F32) for k in range(1, n_z)], pairs[0].astype(F32)
    )
    dnormed = columns[:own_width]
    tail = columns[own_width:]
    plain = (tail[0] + tail[1]) / width
    cross = (tail[2] + tail[3]) / width

    column_start = lax.axis_index(COLS) * own_width
    gain_own = lax.dynamic_slice_in_dim(gain, column_start, own_width, 0)[:, None]
    xhat_own = (own_t.astype(F32) - mean) * inv
    hidden = (inv * (dnormed * gain_own - plain - xhat_own * cross)).astype(BF16).T
    sums = jnp.concatenate([jnp.sum(dnormed * xhat_own, 1), jnp.sum(dnormed, 1)])
    sums, grad_weight = lax.optimization_barrier((sums, grad_weight))
    sums = jnp.sum(copies(sums[None], ENC), (0, 1))
    return embeds_recv, hidden, grad_weight, sums[:own_width], sums[own_width:]


def solution(mesh):
    devices = mesh.devices
    split = Mesh(devices.reshape(8, 4, 4, 2, 2), ("y", "x", "zl", "co", "zh"))
    spec = P(ENC, COLS)
    in_specs = (spec, P(), P(), spec, P(ENC, None), spec)
    out_specs = (spec, spec, spec, P(COLS), P(COLS))
    return jax.shard_map(body, mesh=split, in_specs=in_specs, out_specs=out_specs, check_vma=False)
```

```python
import functools

import jax
import jax.numpy as jnp
from jax import lax
from jax.experimental import pallas as pl
from jax.experimental.pallas import tpu as pltpu
from jax.sharding import Mesh
from jax.sharding import PartitionSpec as P

ENC = ("y", "x")
COLS = ("zl", "co", "zh")
EPSILON = 1e-05
F32 = jnp.float32
BF16 = jnp.bfloat16
VMEM = pl.BlockSpec(memory_space=pltpu.VMEM)
SMEM = pl.BlockSpec(memory_space=pltpu.SMEM)
PARAMS = pltpu.CompilerParams(vmem_limit_bytes=48 * 1024 * 1024)
EXTRA = 8


def exchange(x, axes):
    return lax.all_to_all(x, axes, 0, 0, tiled=True)


def copies(x, axes):
    count = lax.axis_size(axes)
    return exchange(jnp.broadcast_to(x[None], (count, *x.shape)), axes)


def shifted(x, axes, step):
    count = lax.axis_size(axes)
    return lax.ppermute(x, axes, [(i, (i + step) % count) for i in range(count)])


def along_z(x, step):
    n_zl, n_zh = lax.axis_size("zl"), lax.axis_size("zh")
    count = n_zl * n_zh
    at = [(z % n_zl) * n_zh + z // n_zl for z in range(count)]
    return lax.ppermute(x, ("zl", "zh"), [(at[z], at[(z + step) % count]) for z in range(count)])


def core_swap(x):
    return lax.ppermute(x, "co", [(0, 1), (1, 0)])


def block_of(i, core, n_zh):
    return (i // n_zh) * (2 * n_zh) + core * n_zh + i % n_zh


def wide(column, rows):
    return jnp.concatenate([column] * (rows // column.shape[1]), 1)


def norm_kernel(n_zh, place, mine, other, gain, shift, normed, stats):
    core = place[1]
    n_z, own_width, rows = mine.shape
    width = 2 * n_z * own_width

    def totals(i, carry):
        total, squares = carry
        for ref in (mine, other):
            x = ref[i].astype(F32)
            total = total + jnp.sum(x, 0, keepdims=True)
            squares = squares + jnp.sum(x * x, 0, keepdims=True)
        return total, squares

    zero = jnp.zeros((1, rows), F32)
    total, squares = lax.fori_loop(0, n_z, totals, (zero, zero))
    mean = total / width
    inv = lax.rsqrt(squares / width - mean * mean + EPSILON)
    stats[0:1, :] = mean
    stats[1:2, :] = inv
    for i in range(n_z):
        for ref, owner in ((mine, core), (other, 1 - core)):
            b = block_of(i, owner, n_zh)
            value = (ref[i].astype(F32) - mean) * inv * wide(gain[b], rows) + wide(shift[b], rows)
            normed[b] = value.astype(BF16)


def high_low(plain, cross):
    high_plain, high_cross = plain.astype(BF16).astype(F32), cross.astype(BF16).astype(F32)
    pad = jnp.zeros((EXTRA - 4, plain.shape[1]), F32)
    return jnp.concatenate(
        [high_plain, plain - high_plain, high_cross, cross - high_cross, pad], 0
    ).astype(BF16)


def part_kernel(n_zh, place, weight, d_embed, mine, other, gain, stats, keep, send):
    core = place[1]
    n_z, own_width, rows = mine.shape
    mean, inv = stats[0:1, :], stats[1:2, :]
    plain = cross = jnp.zeros((1, rows), F32)
    for i in range(n_z):
        for source, owner, out in ((mine, core, keep), (other, 1 - core, send)):
            b = block_of(i, owner, n_zh)
            part = lax.dot_general(
                weight[b], d_embed[...], (((1,), (1,)), ((), ())), preferred_element_type=F32
            ).astype(BF16)
            out[i, 0:own_width, :] = part
            scaled = part.astype(F32) * wide(gain[b], rows)
            xhat = (source[i].astype(F32) - mean) * inv
            plain = plain + jnp.sum(scaled, 0, keepdims=True)
            cross = cross + jnp.sum(scaled * xhat, 0, keepdims=True)
    tail = high_low(plain, cross)
    for i in range(n_z):
        keep[i, own_width:, :] = tail
        send[i, own_width:, :] = tail


def pair_kernel(n_zl, n_zh, place, keep, recv, *outs):
    n_z, own_width = keep.shape[0], keep.shape[1] - EXTRA
    tail = keep[0, own_width:, :].astype(F32) + recv[0, own_width:, :].astype(F32)
    tail = high_low(tail[0:1] + tail[1:2], tail[2:3] + tail[3:4])
    for k, out in enumerate(outs):
        target = lax.rem(place[0] + k, n_z)
        i = lax.rem(target, n_zl) * n_zh + target // n_zl
        pair = keep[i, 0:own_width, :].astype(F32) + recv[i, 0:own_width, :].astype(F32)
        out[0:own_width, :] = pair.astype(BF16)
        out[own_width:, :] = tail


def body(patches, gain, shift, proj_weight, llm_rank, embed_grad):
    rows, own_width = patches.shape
    width = gain.shape[0]
    out_cols = proj_weight.shape[1]
    n_y, n_x = lax.axis_size("y"), lax.axis_size("x")
    n_zl, n_zh = lax.axis_size("zl"), lax.axis_size("zh")
    n_z = n_zl * n_zh
    senders = n_y * n_x
    slice_rows = proj_weight.shape[0]
    most = embed_grad.shape[0] // senders
    blocks = width // own_width
    core, x_at = lax.axis_index("co"), lax.axis_index("x")
    place = jnp.stack([lax.axis_index("zh") * n_zl + lax.axis_index("zl"), core]).astype(jnp.int32)

    own_t = patches.T
    mine = copies(own_t, ("zl", "zh"))
    other = core_swap(mine)

    weight_rel = [proj_weight] + [shifted(proj_weight, "x", k) for k in range(1, n_x)]
    ordered = jnp.stack([weight_rel[-i % n_x] for i in range(n_x)] * 2)
    weight_x = lax.dynamic_slice_in_dim(ordered, lax.rem(n_x - x_at, n_x), n_x, 0)
    weight = lax.all_gather(weight_x.reshape(n_x * slice_rows, out_cols), "y", axis=0, tiled=True)

    embed_grad, mine = lax.optimization_barrier((embed_grad, mine))
    returned = exchange(embed_grad.reshape(senders, most, out_cols), ENC)

    gain_wide = jnp.broadcast_to(gain.reshape(blocks, own_width, 1), (blocks, own_width, 128))
    shift_wide = jnp.broadcast_to(shift.reshape(blocks, own_width, 1), (blocks, own_width, 128))
    normed, stats = pl.pallas_call(
        functools.partial(norm_kernel, n_zh),
        out_shape=(
            jax.ShapeDtypeStruct((blocks, own_width, rows), BF16),
            jax.ShapeDtypeStruct((8, rows), F32),
        ),
        in_specs=[SMEM] + [VMEM] * 4,
        out_specs=(VMEM,) * 2,
        compiler_params=PARAMS,
        name="norm",
    )(place, mine, other, gain_wide, shift_wide)
    mean, inv = stats[0], stats[1]
    normed = normed.reshape(width, rows)

    target = llm_rank[:, 0]
    owners = jnp.arange(senders, dtype=jnp.int32)
    hits = (target[:, None] == owners[None, :]).astype(jnp.int32)
    rank = jnp.sum((jnp.cumsum(hits, 0) - hits) * hits, 1)
    slot = target * most + rank
    d_embed = returned.reshape(senders * most, out_cols)[slot]

    grad_part = jnp.dot(normed, d_embed, preferred_element_type=F32).astype(BF16)
    grad_y = lax.psum_scatter(grad_part, "y", scatter_dimension=0, tiled=True)
    grad_y = grad_y.reshape(n_x, slice_rows, out_cols)

    def grad_block(step):
        return lax.dynamic_index_in_dim(grad_y, lax.rem(x_at + step, n_x), 0, keepdims=False)

    grad_weight = sum(
        [shifted(grad_block(k), "x", k).astype(F32) for k in range(1, n_x)],
        grad_block(0).astype(F32),
    )

    half_shape = jax.ShapeDtypeStruct((n_z, own_width + EXTRA, rows), BF16)
    keep, send = pl.pallas_call(
        functools.partial(part_kernel, n_zh),
        out_shape=(half_shape, half_shape),
        in_specs=[SMEM] + [VMEM] * 6,
        out_specs=(VMEM,) * 2,
        compiler_params=PARAMS,
        name="part",
    )(place, weight.reshape(blocks, own_width, out_cols), d_embed, mine, other, gain_wide, stats)
    recv = core_swap(send)

    weight_after, keep = lax.optimization_barrier((weight, keep))
    embed = lax.dot_general(
        normed, weight_after, (((0,), (0,)), ((), ())), preferred_element_type=F32
    ).astype(BF16)
    outgoing = jnp.zeros((senders * most, out_cols), BF16).at[slot].set(embed)
    embeds_recv = exchange(outgoing.reshape(senders, most, out_cols), ENC).reshape(
        senders * most, out_cols
    )

    pairs = pl.pallas_call(
        functools.partial(pair_kernel, n_zl, n_zh),
        out_shape=(jax.ShapeDtypeStruct((own_width + EXTRA, rows), BF16),) * n_z,
        in_specs=[SMEM] + [VMEM] * 2,
        out_specs=(VMEM,) * n_z,
        compiler_params=PARAMS,
        name="pair",
    )(place, keep, recv)
    columns = sum(
        [along_z(pairs[k], k).astype(F32) for k in range(1, n_z)], pairs[0].astype(F32)
    )
    dnormed = columns[:own_width]
    tail = columns[own_width:]
    plain = (tail[0] + tail[1]) / width
    cross = (tail[2] + tail[3]) / width

    column_start = lax.axis_index(COLS) * own_width
    gain_own = lax.dynamic_slice_in_dim(gain, column_start, own_width, 0)[:, None]
    xhat_own = (own_t.astype(F32) - mean) * inv
    hidden = (inv * (dnormed * gain_own - plain - xhat_own * cross)).astype(BF16).T
    sums = jnp.concatenate([jnp.sum(dnormed * xhat_own, 1), jnp.sum(dnormed, 1)])
    sums, embeds_recv = lax.optimization_barrier((sums, embeds_recv))
    sums = jnp.sum(copies(sums[None], ENC), (0, 1))
    return embeds_recv, hidden, grad_weight, sums[:own_width], sums[own_width:]


def solution(mesh):
    devices = mesh.devices
    split = Mesh(devices.reshape(8, 4, 4, 2, 2), ("y", "x", "zl", "co", "zh"))
    spec = P(ENC, COLS)
    in_specs = (spec, P(), P(), spec, P(ENC, None), spec)
    out_specs = (spec, spec, spec, P(COLS), P(COLS))
    return jax.shard_map(body, mesh=split, in_specs=in_specs, out_specs=out_specs, check_vma=False)
```

```python
import functools

import jax
import jax.numpy as jnp
from jax import lax
from jax.experimental import pallas as pl
from jax.experimental.pallas import tpu as pltpu
from jax.sharding import Mesh
from jax.sharding import PartitionSpec as P

ENC = ("y", "x")
COLS = ("zl", "co", "zh")
ZED = ("zh", "zl")
EPSILON = 1e-05
F32 = jnp.float32
BF16 = jnp.bfloat16
VMEM = pl.BlockSpec(memory_space=pltpu.VMEM)
SMEM = pl.BlockSpec(memory_space=pltpu.SMEM)
PARAMS = pltpu.CompilerParams(vmem_limit_bytes=48 * 1024 * 1024)
EXTRA = 8


def exchange(x, axes):
    return lax.all_to_all(x, axes, 0, 0, tiled=True)


def copies(x, axes):
    count = lax.axis_size(axes)
    return exchange(jnp.broadcast_to(x[None], (count, *x.shape)), axes)


def shifted(x, axes, step):
    count = lax.axis_size(axes)
    return lax.ppermute(x, axes, [(i, (i + step) % count) for i in range(count)])


def core_swap(x):
    return lax.ppermute(x, "co", [(0, 1), (1, 0)])


def block_of(z, core, n_zl, n_zh):
    return (z % n_zl) * (2 * n_zh) + core * n_zh + z // n_zl


def wide(column, rows):
    return jnp.concatenate([column] * (rows // column.shape[1]), 1)


def norm_kernel(n_zl, n_zh, core_at, mine, other, gain, shift, normed, stats):
    core = core_at[0]
    n_z, own_width, rows = mine.shape
    width = 2 * n_z * own_width

    def totals(i, carry):
        total, squares = carry
        for ref in (mine, other):
            x = ref[i].astype(F32)
            total = total + jnp.sum(x, 0, keepdims=True)
            squares = squares + jnp.sum(x * x, 0, keepdims=True)
        return total, squares

    zero = jnp.zeros((1, rows), F32)
    total, squares = lax.fori_loop(0, n_z, totals, (zero, zero))
    mean = total / width
    inv = lax.rsqrt(squares / width - mean * mean + EPSILON)
    stats[0:1, :] = mean
    stats[1:2, :] = inv
    for i in range(n_z):
        for ref, owner in ((mine, core), (other, 1 - core)):
            b = block_of(i, owner, n_zl, n_zh)
            value = (ref[i].astype(F32) - mean) * inv * wide(gain[b], rows) + wide(shift[b], rows)
            normed[b] = value.astype(BF16)


def high_low(plain, cross):
    high_plain, high_cross = plain.astype(BF16).astype(F32), cross.astype(BF16).astype(F32)
    pad = jnp.zeros((EXTRA - 4, plain.shape[1]), F32)
    return jnp.concatenate(
        [high_plain, plain - high_plain, high_cross, cross - high_cross, pad], 0
    ).astype(BF16)


def part_kernel(n_zl, n_zh, core_at, weight_a, weight_b, d_embed, mine, other, gain, stats, keep, send):
    core = core_at[0]
    n_z, own_width, rows = mine.shape
    mean, inv = stats[0:1, :], stats[1:2, :]
    plain = cross = jnp.zeros((1, rows), F32)
    for i in range(n_z):
        for source, owner, out in ((mine, core, keep), (other, 1 - core, send)):
            b = block_of(i, owner, n_zl, n_zh)
            part = sum(
                lax.dot_general(
                    weight[b], d_embed[h], (((1,), (1,)), ((), ())), preferred_element_type=F32
                )
                for h, weight in enumerate((weight_a, weight_b))
            ).astype(BF16)
            out[i, 0:own_width, :] = part
            scaled = part.astype(F32) * wide(gain[b], rows)
            xhat = (source[i].astype(F32) - mean) * inv
            plain = plain + jnp.sum(scaled, 0, keepdims=True)
            cross = cross + jnp.sum(scaled * xhat, 0, keepdims=True)
    tail = high_low(plain, cross)
    for i in range(n_z):
        keep[i, own_width:, :] = tail
        send[i, own_width:, :] = tail


def pair_kernel(keep, recv, out):
    n_z, own_width = keep.shape[0], keep.shape[1] - EXTRA
    tail = keep[0, own_width:, :].astype(F32) + recv[0, own_width:, :].astype(F32)
    tail = high_low(tail[0:1] + tail[1:2], tail[2:3] + tail[3:4])
    for i in range(n_z):
        pair = keep[i, 0:own_width, :].astype(F32) + recv[i, 0:own_width, :].astype(F32)
        out[i, 0:own_width, :] = pair.astype(BF16)
        out[i, own_width:, :] = tail


def body(patches, gain, shift, proj_weight, llm_rank, embed_grad):
    rows, own_width = patches.shape
    width = gain.shape[0]
    out_cols = proj_weight.shape[1]
    n_y, n_x = lax.axis_size("y"), lax.axis_size("x")
    n_zl, n_zh = lax.axis_size("zl"), lax.axis_size("zh")
    n_z = n_zl * n_zh
    senders = n_y * n_x
    slice_rows = proj_weight.shape[0]
    most = embed_grad.shape[0] // senders
    blocks = width // own_width
    core, x_at = lax.axis_index("co"), lax.axis_index("x")
    core_at = core.astype(jnp.int32).reshape(1)
    half = out_cols // 2

    weight_rel = [proj_weight] + [shifted(proj_weight, "x", k) for k in range(1, n_x)]
    ordered = jnp.stack([weight_rel[-i % n_x] for i in range(n_x)] * 2)
    weight_x = lax.dynamic_slice_in_dim(ordered, lax.rem(n_x - x_at, n_x), n_x, 0)
    weight_x = weight_x.reshape(n_x * slice_rows, out_cols)
    weights = [
        lax.all_gather(weight_x[:, h * half : (h + 1) * half], "y", axis=0, tiled=True)
        for h in range(2)
    ]

    returned = exchange(embed_grad.reshape(senders, most, out_cols), ENC)
    own_t = patches.T
    own_t, _ = lax.optimization_barrier((own_t, weight_x))
    mine = lax.all_gather(own_t, ZED, axis=0)
    other = core_swap(mine)

    gain_wide = jnp.broadcast_to(gain.reshape(blocks, own_width, 1), (blocks, own_width, 128))
    shift_wide = jnp.broadcast_to(shift.reshape(blocks, own_width, 1), (blocks, own_width, 128))
    normed, stats = pl.pallas_call(
        functools.partial(norm_kernel, n_zl, n_zh),
        out_shape=(
            jax.ShapeDtypeStruct((blocks, own_width, rows), BF16),
            jax.ShapeDtypeStruct((8, rows), F32),
        ),
        in_specs=[SMEM] + [VMEM] * 4,
        out_specs=(VMEM,) * 2,
        compiler_params=PARAMS,
        name="norm",
    )(core_at, mine, other, gain_wide, shift_wide)
    mean, inv = stats[0], stats[1]
    normed = normed.reshape(width, rows)

    target = llm_rank[:, 0]
    owners = jnp.arange(senders, dtype=jnp.int32)
    hits = (target[:, None] == owners[None, :]).astype(jnp.int32)
    rank = jnp.sum((jnp.cumsum(hits, 0) - hits) * hits, 1)
    slot = target * most + rank
    d_embed = returned.reshape(senders * most, out_cols)[slot]
    d_halves = [d_embed[:, h * half : (h + 1) * half] for h in range(2)]

    grad_ys = []
    for h in range(2):
        grad_part = jnp.dot(normed, d_halves[h], preferred_element_type=F32).astype(BF16)
        grad_ys.append(lax.psum_scatter(grad_part, "y", scatter_dimension=0, tiled=True))

    def outgoing(h):
        embed = lax.dot_general(
            normed, weights[h], (((0,), (0,)), ((), ())), preferred_element_type=F32
        ).astype(BF16)
        placed = jnp.zeros((senders * most, half), BF16).at[slot].set(embed)
        return placed.reshape(senders, most, half)

    first, _ = lax.optimization_barrier((outgoing(0), d_embed))
    first = exchange(first, ENC)
    second, first = lax.optimization_barrier((outgoing(1), first))
    second = exchange(second, ENC)

    half_shape = jax.ShapeDtypeStruct((n_z, own_width + EXTRA, rows), BF16)
    keep, send = pl.pallas_call(
        functools.partial(part_kernel, n_zl, n_zh),
        out_shape=(half_shape, half_shape),
        in_specs=[SMEM] + [VMEM] * 7,
        out_specs=(VMEM,) * 2,
        compiler_params=PARAMS,
        name="part",
    )(
        core_at,
        weights[0].reshape(blocks, own_width, half),
        weights[1].reshape(blocks, own_width, half),
        jnp.stack(d_halves),
        mine,
        other,
        gain_wide,
        stats,
    )
    pairs = pl.pallas_call(
        pair_kernel,
        out_shape=half_shape,
        in_specs=[VMEM] * 2,
        out_specs=VMEM,
        compiler_params=PARAMS,
        name="pair",
    )(keep, core_swap(send))
    pairs, second = lax.optimization_barrier((pairs, second))
    columns = jnp.sum(exchange(pairs, ZED).astype(F32), 0)
    dnormed = columns[:own_width]
    tail = columns[own_width:]
    plain = (tail[0] + tail[1]) / width
    cross = (tail[2] + tail[3]) / width

    column_start = lax.axis_index(COLS) * own_width
    gain_own = lax.dynamic_slice_in_dim(gain, column_start, own_width, 0)[:, None]
    xhat_own = (own_t.astype(F32) - mean) * inv
    hidden = (inv * (dnormed * gain_own - plain - xhat_own * cross)).astype(BF16).T
    sums = jnp.concatenate([jnp.sum(dnormed * xhat_own, 1), jnp.sum(dnormed, 1)])
    grad_ys[1], sums = lax.optimization_barrier((grad_ys[1], sums))
    sums = jnp.sum(copies(sums[None], ENC), (0, 1))

    def reduced(grad_y):
        grad_y = grad_y.reshape(n_x, slice_rows, half)

        def block(step):
            return lax.dynamic_index_in_dim(grad_y, lax.rem(x_at + step, n_x), 0, keepdims=False)

        return sum(
            [shifted(block(k), "x", k).astype(F32) for k in range(1, n_x)], block(0).astype(F32)
        )

    grad_weight = jnp.concatenate([reduced(grad_y) for grad_y in grad_ys], 1)
    embeds_recv = jnp.concatenate([first, second], 2).reshape(senders * most, out_cols)
    return embeds_recv, hidden, grad_weight, sums[:own_width], sums[own_width:]


def solution(mesh):
    devices = mesh.devices
    split = Mesh(devices.reshape(8, 4, 4, 2, 2), ("y", "x", "zl", "co", "zh"))
    spec = P(ENC, COLS)
    in_specs = (spec, P(), P(), spec, P(ENC, None), spec)
    out_specs = (spec, spec, spec, P(COLS), P(COLS))
    return jax.shard_map(body, mesh=split, in_specs=in_specs, out_specs=out_specs, check_vma=False)
```

```python
import functools

import jax
import jax.numpy as jnp
from jax import lax
from jax.experimental import pallas as pl
from jax.experimental.pallas import tpu as pltpu
from jax.sharding import Mesh
from jax.sharding import PartitionSpec as P

ENC = ("y", "x")
COLS = ("zl", "co", "zh")
ZED = ("zh", "zl")
EPSILON = 1e-05
F32 = jnp.float32
BF16 = jnp.bfloat16
VMEM = pl.BlockSpec(memory_space=pltpu.VMEM)
SMEM = pl.BlockSpec(memory_space=pltpu.SMEM)
PARAMS = pltpu.CompilerParams(vmem_limit_bytes=48 * 1024 * 1024)
EXTRA = 8


def exchange(x, axes):
    return lax.all_to_all(x, axes, 0, 0, tiled=True)


def copies(x, axes):
    count = lax.axis_size(axes)
    return exchange(jnp.broadcast_to(x[None], (count, *x.shape)), axes)


def shifted(x, axes, step):
    count = lax.axis_size(axes)
    return lax.ppermute(x, axes, [(i, (i + step) % count) for i in range(count)])


def along_z(x, step):
    n_zl, n_zh = lax.axis_size("zl"), lax.axis_size("zh")
    count = n_zl * n_zh
    at = [(z % n_zl) * n_zh + z // n_zl for z in range(count)]
    return lax.ppermute(x, ("zl", "zh"), [(at[z], at[(z + step) % count]) for z in range(count)])


def core_swap(x):
    return lax.ppermute(x, "co", [(0, 1), (1, 0)])


def block_of(z, core, n_zl, n_zh):
    return (z % n_zl) * (2 * n_zh) + core * n_zh + z // n_zl


def wide(column, rows):
    return jnp.concatenate([column] * (rows // column.shape[1]), 1)


def norm_kernel(n_zl, n_zh, at, mine, other, gain, shift, normed, stats):
    core = at[0]
    n_z, own_width, rows = mine.shape
    width = 2 * n_z * own_width

    def totals(i, carry):
        total, squares = carry
        for ref in (mine, other):
            x = ref[i].astype(F32)
            total = total + jnp.sum(x, 0, keepdims=True)
            squares = squares + jnp.sum(x * x, 0, keepdims=True)
        return total, squares

    zero = jnp.zeros((1, rows), F32)
    total, squares = lax.fori_loop(0, n_z, totals, (zero, zero))
    mean = total / width
    inv = lax.rsqrt(squares / width - mean * mean + EPSILON)
    stats[0:1, :] = mean
    stats[1:2, :] = inv
    for i in range(n_z):
        for ref, owner in ((mine, core), (other, 1 - core)):
            b = block_of(i, owner, n_zl, n_zh)
            value = (ref[i].astype(F32) - mean) * inv * wide(gain[b], rows) + wide(shift[b], rows)
            normed[b] = value.astype(BF16)


def high_low(plain, cross):
    high_plain, high_cross = plain.astype(BF16).astype(F32), cross.astype(BF16).astype(F32)
    pad = jnp.zeros((EXTRA - 4, plain.shape[1]), F32)
    return jnp.concatenate(
        [high_plain, plain - high_plain, high_cross, cross - high_cross, pad], 0
    ).astype(BF16)


def part_kernel(n_zl, n_zh, at, weight, d_embed, mine, other, gain, stats, keep, send):
    core = at[0]
    n_z, own_width, rows = mine.shape
    mean, inv = stats[0:1, :], stats[1:2, :]
    plain = cross = jnp.zeros((1, rows), F32)
    for i in range(n_z):
        for source, owner, out in ((mine, core, keep), (other, 1 - core, send)):
            b = block_of(i, owner, n_zl, n_zh)
            part = lax.dot_general(
                weight[b], d_embed[...], (((1,), (1,)), ((), ())), preferred_element_type=F32
            ).astype(BF16)
            out[i, 0:own_width, :] = part
            scaled = part.astype(F32) * wide(gain[b], rows)
            xhat = (source[i].astype(F32) - mean) * inv
            plain = plain + jnp.sum(scaled, 0, keepdims=True)
            cross = cross + jnp.sum(scaled * xhat, 0, keepdims=True)
    tail = high_low(plain, cross)
    for i in range(n_z):
        keep[i, own_width:, :] = tail
        send[i, own_width:, :] = tail


def pair_kernel(at, keep, recv, *outs):
    n_z, own_width = keep.shape[0], keep.shape[1] - EXTRA
    tail = keep[0, own_width:, :].astype(F32) + recv[0, own_width:, :].astype(F32)
    tail = high_low(tail[0:1] + tail[1:2], tail[2:3] + tail[3:4])
    for k, out in enumerate(outs):
        i = lax.rem(at[1] + k, n_z)
        pair = keep[i, 0:own_width, :].astype(F32) + recv[i, 0:own_width, :].astype(F32)
        out[0:own_width, :] = pair.astype(BF16)
        out[own_width:, :] = tail


def body(patches, gain, shift, proj_weight, llm_rank, embed_grad):
    rows, own_width = patches.shape
    width = gain.shape[0]
    out_cols = proj_weight.shape[1]
    n_y, n_x = lax.axis_size("y"), lax.axis_size("x")
    n_zl, n_zh = lax.axis_size("zl"), lax.axis_size("zh")
    n_z = n_zl * n_zh
    senders = n_y * n_x
    slice_rows = proj_weight.shape[0]
    most = embed_grad.shape[0] // senders
    blocks = width // own_width
    core, x_at = lax.axis_index("co"), lax.axis_index("x")
    at = jnp.stack([core, lax.axis_index(ZED)]).astype(jnp.int32)

    weight_rel = [proj_weight] + [shifted(proj_weight, "x", k) for k in range(1, n_x)]
    ordered = jnp.stack([weight_rel[-i % n_x] for i in range(n_x)] * 2)
    weight_x = lax.dynamic_slice_in_dim(ordered, lax.rem(n_x - x_at, n_x), n_x, 0)
    weight_x = weight_x.reshape(n_x * slice_rows, out_cols)
    weight = lax.all_gather(weight_x, "y", axis=0, tiled=True)

    returned = exchange(embed_grad.reshape(senders, most, out_cols), ENC)
    own_t = patches.T
    own_t, _ = lax.optimization_barrier((own_t, weight_x))
    mine = lax.all_gather(own_t, ZED, axis=0)
    other = core_swap(mine)

    gain_wide = jnp.broadcast_to(gain.reshape(blocks, own_width, 1), (blocks, own_width, 128))
    shift_wide = jnp.broadcast_to(shift.reshape(blocks, own_width, 1), (blocks, own_width, 128))
    normed, stats = pl.pallas_call(
        functools.partial(norm_kernel, n_zl, n_zh),
        out_shape=(
            jax.ShapeDtypeStruct((blocks, own_width, rows), BF16),
            jax.ShapeDtypeStruct((8, rows), F32),
        ),
        in_specs=[SMEM] + [VMEM] * 4,
        out_specs=(VMEM,) * 2,
        compiler_params=PARAMS,
        name="norm",
    )(at, mine, other, gain_wide, shift_wide)
    mean, inv = stats[0], stats[1]
    normed = normed.reshape(width, rows)

    target = llm_rank[:, 0]
    owners = jnp.arange(senders, dtype=jnp.int32)
    hits = (target[:, None] == owners[None, :]).astype(jnp.int32)
    rank = jnp.sum((jnp.cumsum(hits, 0) - hits) * hits, 1)
    slot = target * most + rank
    d_embed = returned.reshape(senders * most, out_cols)[slot]

    grad_part = jnp.dot(normed, d_embed, preferred_element_type=F32).astype(BF16)
    grad_y = lax.psum_scatter(grad_part, "y", scatter_dimension=0, tiled=True)

    half_shape = jax.ShapeDtypeStruct((n_z, own_width + EXTRA, rows), BF16)
    keep, send = pl.pallas_call(
        functools.partial(part_kernel, n_zl, n_zh),
        out_shape=(half_shape, half_shape),
        in_specs=[SMEM] + [VMEM] * 6,
        out_specs=(VMEM,) * 2,
        compiler_params=PARAMS,
        name="part",
    )(
        at, weight.reshape(blocks, own_width, out_cols), d_embed, mine, other, gain_wide, stats
    )
    recv = core_swap(send)

    weight_after, keep = lax.optimization_barrier((weight, keep))
    embed = lax.dot_general(
        normed, weight_after, (((0,), (0,)), ((), ())), preferred_element_type=F32
    ).astype(BF16)
    outgoing = jnp.zeros((senders * most, out_cols), BF16).at[slot].set(embed)
    embeds_recv = exchange(outgoing.reshape(senders, most, out_cols), ENC).reshape(
        senders * most, out_cols
    )

    pairs = pl.pallas_call(
        pair_kernel,
        out_shape=(jax.ShapeDtypeStruct((own_width + EXTRA, rows), BF16),) * n_z,
        in_specs=[SMEM] + [VMEM] * 2,
        out_specs=(VMEM,) * n_z,
        compiler_params=PARAMS,
        name="pair",
    )(at, keep, recv)
    columns = sum(
        [along_z(pairs[k], k).astype(F32) for k in range(1, n_z)], pairs[0].astype(F32)
    )
    dnormed = columns[:own_width]
    tail = columns[own_width:]
    plain = (tail[0] + tail[1]) / width
    cross = (tail[2] + tail[3]) / width

    column_start = lax.axis_index(COLS) * own_width
    gain_own = lax.dynamic_slice_in_dim(gain, column_start, own_width, 0)[:, None]
    xhat_own = (own_t.astype(F32) - mean) * inv
    hidden = (inv * (dnormed * gain_own - plain - xhat_own * cross)).astype(BF16).T
    sums = jnp.concatenate([jnp.sum(dnormed * xhat_own, 1), jnp.sum(dnormed, 1)])
    grad_y, sums = lax.optimization_barrier((grad_y, sums))
    sums, embeds_recv = lax.optimization_barrier((sums, embeds_recv))
    sums = jnp.sum(copies(sums[None], ENC), (0, 1))

    grad_y = grad_y.reshape(n_x, slice_rows, out_cols)

    def grad_block(step):
        return lax.dynamic_index_in_dim(grad_y, lax.rem(x_at + step, n_x), 0, keepdims=False)

    grad_weight = sum(
        [shifted(grad_block(k), "x", k).astype(F32) for k in range(1, n_x)],
        grad_block(0).astype(F32),
    )
    return embeds_recv, hidden, grad_weight, sums[:own_width], sums[own_width:]


def solution(mesh):
    devices = mesh.devices
    split = Mesh(devices.reshape(8, 4, 4, 2, 2), ("y", "x", "zl", "co", "zh"))
    spec = P(ENC, COLS)
    in_specs = (spec, P(), P(), spec, P(ENC, None), spec)
    out_specs = (spec, spec, spec, P(COLS), P(COLS))
    return jax.shard_map(body, mesh=split, in_specs=in_specs, out_specs=out_specs, check_vma=False)
```

```python
import functools

import jax
import jax.numpy as jnp
from jax import lax
from jax.experimental import pallas as pl
from jax.experimental.pallas import tpu as pltpu
from jax.sharding import Mesh
from jax.sharding import PartitionSpec as P

ENC = ("y", "x")
COLS = ("zl", "co", "zh")
ZED = ("zh", "zl")
EPSILON = 1e-05
F32 = jnp.float32
BF16 = jnp.bfloat16
VMEM = pl.BlockSpec(memory_space=pltpu.VMEM)
SMEM = pl.BlockSpec(memory_space=pltpu.SMEM)
PARAMS = pltpu.CompilerParams(vmem_limit_bytes=48 * 1024 * 1024)
EXTRA = 8


def exchange(x, axes):
    return lax.all_to_all(x, axes, 0, 0, tiled=True)


def copies(x, axes):
    count = lax.axis_size(axes)
    return exchange(jnp.broadcast_to(x[None], (count, *x.shape)), axes)


def shifted(x, axes, step):
    count = lax.axis_size(axes)
    return lax.ppermute(x, axes, [(i, (i + step) % count) for i in range(count)])


def along_z(x, step):
    n_zl, n_zh = lax.axis_size("zl"), lax.axis_size("zh")
    count = n_zl * n_zh
    at = [(z % n_zl) * n_zh + z // n_zl for z in range(count)]
    return lax.ppermute(x, ("zl", "zh"), [(at[z], at[(z + step) % count]) for z in range(count)])


def core_swap(x):
    return lax.ppermute(x, "co", [(0, 1), (1, 0)])


def block_of(z, core, n_zl, n_zh):
    return (z % n_zl) * (2 * n_zh) + core * n_zh + z // n_zl


def wide(column, rows):
    return jnp.concatenate([column] * (rows // column.shape[1]), 1)


def norm_kernel(n_zl, n_zh, at, mine, other, gain, shift, normed, stats):
    core = at[0]
    n_z, own_width, rows = mine.shape
    width = 2 * n_z * own_width

    def totals(i, carry):
        total, squares = carry
        for ref in (mine, other):
            x = ref[i].astype(F32)
            total = total + jnp.sum(x, 0, keepdims=True)
            squares = squares + jnp.sum(x * x, 0, keepdims=True)
        return total, squares

    zero = jnp.zeros((1, rows), F32)
    total, squares = lax.fori_loop(0, n_z, totals, (zero, zero))
    mean = total / width
    inv = lax.rsqrt(squares / width - mean * mean + EPSILON)
    stats[0:1, :] = mean
    stats[1:2, :] = inv
    for i in range(n_z):
        for ref, owner in ((mine, core), (other, 1 - core)):
            b = block_of(i, owner, n_zl, n_zh)
            value = (ref[i].astype(F32) - mean) * inv * wide(gain[b], rows) + wide(shift[b], rows)
            normed[b] = value.astype(BF16)


def high_low(plain, cross):
    high_plain, high_cross = plain.astype(BF16).astype(F32), cross.astype(BF16).astype(F32)
    pad = jnp.zeros((EXTRA - 4, plain.shape[1]), F32)
    return jnp.concatenate(
        [high_plain, plain - high_plain, high_cross, cross - high_cross, pad], 0
    ).astype(BF16)


def part_kernel(n_zl, n_zh, at, weight, d_embed, mine, other, gain, stats, keep, send):
    core = at[0]
    n_z, own_width, rows = mine.shape
    mean, inv = stats[0:1, :], stats[1:2, :]
    plain = cross = jnp.zeros((1, rows), F32)
    for i in range(n_z):
        for source, owner, out in ((mine, core, keep), (other, 1 - core, send)):
            b = block_of(i, owner, n_zl, n_zh)
            part = lax.dot_general(
                weight[b], d_embed[...], (((1,), (1,)), ((), ())), preferred_element_type=F32
            ).astype(BF16)
            out[i, 0:own_width, :] = part
            scaled = part.astype(F32) * wide(gain[b], rows)
            xhat = (source[i].astype(F32) - mean) * inv
            plain = plain + jnp.sum(scaled, 0, keepdims=True)
            cross = cross + jnp.sum(scaled * xhat, 0, keepdims=True)
    tail = high_low(plain, cross)
    for i in range(n_z):
        keep[i, own_width:, :] = tail
        send[i, own_width:, :] = tail


def pair_kernel(at, keep, recv, *outs):
    n_z, own_width = keep.shape[0], keep.shape[1] - EXTRA
    tail = keep[0, own_width:, :].astype(F32) + recv[0, own_width:, :].astype(F32)
    tail = high_low(tail[0:1] + tail[1:2], tail[2:3] + tail[3:4])
    for k, out in enumerate(outs):
        i = lax.rem(at[1] + k, n_z)
        pair = keep[i, 0:own_width, :].astype(F32) + recv[i, 0:own_width, :].astype(F32)
        out[0:own_width, :] = pair.astype(BF16)
        out[own_width:, :] = tail


def body(patches, gain, shift, proj_weight, llm_rank, embed_grad):
    rows, own_width = patches.shape
    width = gain.shape[0]
    out_cols = proj_weight.shape[1]
    n_y, n_x = lax.axis_size("y"), lax.axis_size("x")
    n_zl, n_zh = lax.axis_size("zl"), lax.axis_size("zh")
    n_z = n_zl * n_zh
    senders = n_y * n_x
    slice_rows = proj_weight.shape[0]
    padded_rows = (slice_rows + 2 + 7) // 8 * 8
    most = embed_grad.shape[0] // senders
    blocks = width // own_width
    core, x_at = lax.axis_index("co"), lax.axis_index("x")
    at = jnp.stack([core, lax.axis_index(ZED)]).astype(jnp.int32)

    weight_rel = [proj_weight] + [shifted(proj_weight, "x", k) for k in range(1, n_x)]
    ordered = jnp.stack([weight_rel[-i % n_x] for i in range(n_x)] * 2)
    weight_x = lax.dynamic_slice_in_dim(ordered, lax.rem(n_x - x_at, n_x), n_x, 0)
    weight_x = weight_x.reshape(n_x * slice_rows, out_cols)
    weight = lax.all_gather(weight_x, "y", axis=0, tiled=True)

    returned = exchange(embed_grad.reshape(senders, most, out_cols), ENC)
    own_t = patches.T
    own_t, _ = lax.optimization_barrier((own_t, weight_x))
    mine = lax.all_gather(own_t, ZED, axis=0)
    other = core_swap(mine)

    gain_wide = jnp.broadcast_to(gain.reshape(blocks, own_width, 1), (blocks, own_width, 128))
    shift_wide = jnp.broadcast_to(shift.reshape(blocks, own_width, 1), (blocks, own_width, 128))
    normed, stats = pl.pallas_call(
        functools.partial(norm_kernel, n_zl, n_zh),
        out_shape=(
            jax.ShapeDtypeStruct((blocks, own_width, rows), BF16),
            jax.ShapeDtypeStruct((8, rows), F32),
        ),
        in_specs=[SMEM] + [VMEM] * 4,
        out_specs=(VMEM,) * 2,
        compiler_params=PARAMS,
        name="norm",
    )(at, mine, other, gain_wide, shift_wide)
    mean, inv = stats[0], stats[1]
    normed = normed.reshape(width, rows)

    target = llm_rank[:, 0]
    owners = jnp.arange(senders, dtype=jnp.int32)
    hits = (target[:, None] == owners[None, :]).astype(jnp.int32)
    rank = jnp.sum((jnp.cumsum(hits, 0) - hits) * hits, 1)
    slot = target * most + rank
    d_embed = returned.reshape(senders * most, out_cols)[slot]

    grad_part = jnp.dot(normed, d_embed, preferred_element_type=F32).astype(BF16)
    grad_y = lax.psum_scatter(grad_part, "y", scatter_dimension=0, tiled=True)

    half_shape = jax.ShapeDtypeStruct((n_z, own_width + EXTRA, rows), BF16)
    keep, send = pl.pallas_call(
        functools.partial(part_kernel, n_zl, n_zh),
        out_shape=(half_shape, half_shape),
        in_specs=[SMEM] + [VMEM] * 6,
        out_specs=(VMEM,) * 2,
        compiler_params=PARAMS,
        name="part",
    )(
        at, weight.reshape(blocks, own_width, out_cols), d_embed, mine, other, gain_wide, stats
    )
    recv = core_swap(send)

    weight_after, keep = lax.optimization_barrier((weight, keep))
    embed = lax.dot_general(
        normed, weight_after, (((0,), (0,)), ((), ())), preferred_element_type=F32
    ).astype(BF16)
    outgoing = jnp.zeros((senders * most, out_cols), BF16).at[slot].set(embed)
    embeds_recv = exchange(outgoing.reshape(senders, most, out_cols), ENC).reshape(
        senders * most, out_cols
    )

    pairs = pl.pallas_call(
        pair_kernel,
        out_shape=(jax.ShapeDtypeStruct((own_width + EXTRA, rows), BF16),) * n_z,
        in_specs=[SMEM] + [VMEM] * 2,
        out_specs=(VMEM,) * n_z,
        compiler_params=PARAMS,
        name="pair",
    )(at, keep, recv)
    columns = sum(
        [along_z(pairs[k], k).astype(F32) for k in range(1, n_z)], pairs[0].astype(F32)
    )
    dnormed = columns[:own_width]
    tail = columns[own_width:]
    plain = (tail[0] + tail[1]) / width
    cross = (tail[2] + tail[3]) / width

    column_start = lax.axis_index(COLS) * own_width
    gain_own = lax.dynamic_slice_in_dim(gain, column_start, own_width, 0)[:, None]
    xhat_own = (own_t.astype(F32) - mean) * inv
    hidden = (inv * (dnormed * gain_own - plain - xhat_own * cross)).astype(BF16).T
    sums = jnp.concatenate([jnp.sum(dnormed * xhat_own, 1), jnp.sum(dnormed, 1)])
    sums, embeds_recv = lax.optimization_barrier((sums, embeds_recv))
    sums = jnp.sum(copies(sums[None], "y"), (0, 1))

    high = lax.reduce_precision(sums, 8, 7)
    tail = jnp.stack([high, sums - high]).astype(BF16)
    tail = jnp.pad(tail, ((0, padded_rows - slice_rows - 2), (0, out_cols - sums.size)))
    grad_y, tail = lax.optimization_barrier((grad_y, tail))
    grad_x = jnp.concatenate(
        [
            grad_y.reshape(n_x, slice_rows, out_cols),
            jnp.broadcast_to(tail[None], (n_x, *tail.shape)),
        ],
        1,
    )
    total = jnp.sum(exchange(grad_x, "x").astype(F32), 0)
    grad_weight = total[:slice_rows]
    sums = total[slice_rows] + total[slice_rows + 1]
    return (
        embeds_recv,
        hidden,
        grad_weight,
        sums[:own_width],
        sums[own_width : 2 * own_width],
    )


def solution(mesh):
    devices = mesh.devices
    split = Mesh(devices.reshape(8, 4, 4, 2, 2), ("y", "x", "zl", "co", "zh"))
    spec = P(ENC, COLS)
    in_specs = (spec, P(), P(), spec, P(ENC, None), spec)
    out_specs = (spec, spec, spec, P(COLS), P(COLS))
    return jax.shard_map(body, mesh=split, in_specs=in_specs, out_specs=out_specs, check_vma=False)
```

```python
import functools

import jax
import jax.numpy as jnp
from jax import lax
from jax.experimental import pallas as pl
from jax.experimental.pallas import tpu as pltpu
from jax.sharding import Mesh
from jax.sharding import PartitionSpec as P

ENC = ("y", "x")
COLS = ("zl", "co", "zh")
ZED = ("zh", "zl")
EPSILON = 1e-05
F32 = jnp.float32
BF16 = jnp.bfloat16
VMEM = pl.BlockSpec(memory_space=pltpu.VMEM)
SMEM = pl.BlockSpec(memory_space=pltpu.SMEM)
PARAMS = pltpu.CompilerParams(vmem_limit_bytes=48 * 1024 * 1024)
EXTRA = 8


def exchange(x, axes):
    return lax.all_to_all(x, axes, 0, 0, tiled=True)


def copies(x, axes):
    count = lax.axis_size(axes)
    return exchange(jnp.broadcast_to(x[None], (count, *x.shape)), axes)


def shifted(x, axes, step):
    count = lax.axis_size(axes)
    return lax.ppermute(x, axes, [(i, (i + step) % count) for i in range(count)])


def along_z(x, step):
    n_zl, n_zh = lax.axis_size("zl"), lax.axis_size("zh")
    count = n_zl * n_zh
    at = [(z % n_zl) * n_zh + z // n_zl for z in range(count)]
    return lax.ppermute(x, ("zl", "zh"), [(at[z], at[(z + step) % count]) for z in range(count)])


def core_swap(x):
    return lax.ppermute(x, "co", [(0, 1), (1, 0)])


def block_of(z, core, n_zl, n_zh):
    return (z % n_zl) * (2 * n_zh) + core * n_zh + z // n_zl


def column(table, z, owner, n_zl, n_zh):
    first = block_of(z, 0, n_zl, n_zh)
    second = block_of(z, 1, n_zl, n_zh)
    return jnp.where(owner == 0, table[:, first : first + 1], table[:, second : second + 1])


def norm_kernel(n_zl, n_zh, at, mine, other, gain, shift, normed, stats):
    core = at[0]
    n_z, own_width, rows = mine.shape
    width = 2 * n_z * own_width

    def totals(i, carry):
        total, squares = carry
        for ref in (mine, other):
            x = ref[i].astype(F32)
            total = total + jnp.sum(x, 0, keepdims=True)
            squares = squares + jnp.sum(x * x, 0, keepdims=True)
        return total, squares

    zero = jnp.zeros((1, rows), F32)
    total, squares = lax.fori_loop(0, n_z, totals, (zero, zero))
    mean = total / width
    inv = lax.rsqrt(squares / width - mean * mean + EPSILON)
    stats[0:1, :] = mean
    stats[1:2, :] = inv
    for i in range(n_z):
        for ref, owner in ((mine, core), (other, 1 - core)):
            b = block_of(i, owner, n_zl, n_zh)
            scale = column(gain, i, owner, n_zl, n_zh)
            offset = column(shift, i, owner, n_zl, n_zh)
            value = (ref[i].astype(F32) - mean) * inv * scale + offset
            normed[b] = value.astype(BF16)


def high_low(plain, cross):
    high_plain, high_cross = plain.astype(BF16).astype(F32), cross.astype(BF16).astype(F32)
    pad = jnp.zeros((EXTRA - 4, plain.shape[1]), F32)
    return jnp.concatenate(
        [high_plain, plain - high_plain, high_cross, cross - high_cross, pad], 0
    ).astype(BF16)


def part_kernel(n_zl, n_zh, at, weight, d_embed, mine, other, gain, stats, keep, send):
    core = at[0]
    n_z, own_width, rows = mine.shape
    mean, inv = stats[0:1, :], stats[1:2, :]
    plain = cross = jnp.zeros((1, rows), F32)
    for i in range(n_z):
        for source, owner, out in ((mine, core, keep), (other, 1 - core, send)):
            b = block_of(i, owner, n_zl, n_zh)
            part = lax.dot_general(
                weight[b], d_embed[...], (((1,), (1,)), ((), ())), preferred_element_type=F32
            ).astype(BF16)
            out[i, 0:own_width, :] = part
            scaled = part.astype(F32) * column(gain, i, owner, n_zl, n_zh)
            xhat = (source[i].astype(F32) - mean) * inv
            plain = plain + jnp.sum(scaled, 0, keepdims=True)
            cross = cross + jnp.sum(scaled * xhat, 0, keepdims=True)
    tail = high_low(plain, cross)
    for i in range(n_z):
        keep[i, own_width:, :] = tail
        send[i, own_width:, :] = tail


def pair_kernel(at, keep, recv, *outs):
    n_z, own_width = keep.shape[0], keep.shape[1] - EXTRA
    tail = keep[0, own_width:, :].astype(F32) + recv[0, own_width:, :].astype(F32)
    tail = high_low(tail[0:1] + tail[1:2], tail[2:3] + tail[3:4])
    for k, out in enumerate(outs):
        i = lax.rem(at[1] + k, n_z)
        pair = keep[i, 0:own_width, :].astype(F32) + recv[i, 0:own_width, :].astype(F32)
        out[0:own_width, :] = pair.astype(BF16)
        out[own_width:, :] = tail


def body(patches, gain, shift, proj_weight, llm_rank, embed_grad):
    rows, own_width = patches.shape
    width = gain.shape[0]
    out_cols = proj_weight.shape[1]
    n_y, n_x = lax.axis_size("y"), lax.axis_size("x")
    n_zl, n_zh = lax.axis_size("zl"), lax.axis_size("zh")
    n_z = n_zl * n_zh
    senders = n_y * n_x
    slice_rows = proj_weight.shape[0]
    padded_rows = (slice_rows + 2 + 7) // 8 * 8
    most = embed_grad.shape[0] // senders
    blocks = width // own_width
    core = lax.axis_index("co")
    at = jnp.stack([core, lax.axis_index(ZED)]).astype(jnp.int32)

    weight_x = copies(proj_weight, "x").reshape(n_x * slice_rows, out_cols)
    weight = lax.all_gather(weight_x, "y", axis=0, tiled=True)

    embed_grad, _ = lax.optimization_barrier((embed_grad, weight_x))
    returned = exchange(embed_grad.reshape(senders, most, out_cols), ENC)
    own_t = patches.T
    own_t, _ = lax.optimization_barrier((own_t, weight_x))
    mine = lax.all_gather(own_t, ZED, axis=0)
    other = core_swap(mine)

    gain_t, shift_t = gain.reshape(blocks, own_width).T, shift.reshape(blocks, own_width).T
    normed, stats = pl.pallas_call(
        functools.partial(norm_kernel, n_zl, n_zh),
        out_shape=(
            jax.ShapeDtypeStruct((blocks, own_width, rows), BF16),
            jax.ShapeDtypeStruct((8, rows), F32),
        ),
        in_specs=[SMEM] + [VMEM] * 4,
        out_specs=(VMEM,) * 2,
        compiler_params=PARAMS,
        name="norm",
    )(at, mine, other, gain_t, shift_t)
    mean, inv = stats[0], stats[1]
    normed = normed.reshape(width, rows)

    target = llm_rank[:, 0]
    owners = jnp.arange(senders, dtype=jnp.int32)
    hits = (target[:, None] == owners[None, :]).astype(jnp.int32)
    rank = jnp.sum((jnp.cumsum(hits, 0) - hits) * hits, 1)
    slot = target * most + rank
    d_embed = returned.reshape(senders * most, out_cols)[slot]

    grad_part = jnp.dot(normed, d_embed, preferred_element_type=F32).astype(BF16)
    grad_y = lax.psum_scatter(grad_part, "y", scatter_dimension=0, tiled=True)

    half_shape = jax.ShapeDtypeStruct((n_z, own_width + EXTRA, rows), BF16)
    keep, send = pl.pallas_call(
        functools.partial(part_kernel, n_zl, n_zh),
        out_shape=(half_shape, half_shape),
        in_specs=[SMEM] + [VMEM] * 6,
        out_specs=(VMEM,) * 2,
        compiler_params=PARAMS,
        name="part",
    )(
        at, weight.reshape(blocks, own_width, out_cols), d_embed, mine, other, gain_t, stats
    )
    recv = core_swap(send)

    weight_after, keep = lax.optimization_barrier((weight, keep))
    embed = lax.dot_general(
        normed, weight_after, (((0,), (0,)), ((), ())), preferred_element_type=F32
    ).astype(BF16)
    outgoing = jnp.zeros((senders * most, out_cols), BF16).at[slot].set(embed)
    embeds_recv = exchange(outgoing.reshape(senders, most, out_cols), ENC).reshape(
        senders * most, out_cols
    )

    pairs = pl.pallas_call(
        pair_kernel,
        out_shape=(jax.ShapeDtypeStruct((own_width + EXTRA, rows), BF16),) * n_z,
        in_specs=[SMEM] + [VMEM] * 2,
        out_specs=(VMEM,) * n_z,
        compiler_params=PARAMS,
        name="pair",
    )(at, keep, recv)
    columns = sum(
        [along_z(pairs[k], k).astype(F32) for k in range(1, n_z)], pairs[0].astype(F32)
    )
    dnormed = columns[:own_width]
    tail = columns[own_width:]
    plain = (tail[0] + tail[1]) / width
    cross = (tail[2] + tail[3]) / width

    column_start = lax.axis_index(COLS) * own_width
    gain_own = lax.dynamic_slice_in_dim(gain, column_start, own_width, 0)[:, None]
    xhat_own = (own_t.astype(F32) - mean) * inv
    hidden = (inv * (dnormed * gain_own - plain - xhat_own * cross)).astype(BF16).T
    sums = jnp.concatenate([jnp.sum(dnormed * xhat_own, 1), jnp.sum(dnormed, 1)])
    sums, embeds_recv = lax.optimization_barrier((sums, embeds_recv))
    sums = jnp.sum(copies(sums[None], "y"), (0, 1))

    high = lax.reduce_precision(sums, 8, 7)
    tail = jnp.stack([high, sums - high]).astype(BF16)
    tail = jnp.pad(tail, ((0, padded_rows - slice_rows - 2), (0, out_cols - sums.size)))
    grad_y, tail = lax.optimization_barrier((grad_y, tail))
    grad_x = jnp.concatenate(
        [
            grad_y.reshape(n_x, slice_rows, out_cols),
            jnp.broadcast_to(tail[None], (n_x, *tail.shape)),
        ],
        1,
    )
    total = jnp.sum(exchange(grad_x, "x").astype(F32), 0)
    grad_weight = total[:slice_rows]
    sums = total[slice_rows] + total[slice_rows + 1]
    return (
        embeds_recv,
        hidden,
        grad_weight,
        sums[:own_width],
        sums[own_width : 2 * own_width],
    )


def solution(mesh):
    devices = mesh.devices
    split = Mesh(devices.reshape(8, 4, 4, 2, 2), ("y", "x", "zl", "co", "zh"))
    spec = P(ENC, COLS)
    in_specs = (spec, P(), P(), spec, P(ENC, None), spec)
    out_specs = (spec, spec, spec, P(COLS), P(COLS))
    return jax.shard_map(body, mesh=split, in_specs=in_specs, out_specs=out_specs, check_vma=False)
```

```python
import functools

import jax
import jax.numpy as jnp
from jax import lax
from jax.experimental import pallas as pl
from jax.experimental.pallas import tpu as pltpu
from jax.sharding import Mesh
from jax.sharding import PartitionSpec as P

ENC = ("y", "x")
COLS = ("zl", "co", "zh")
ZED = ("zh", "zl")
EPSILON = 1e-05
F32 = jnp.float32
BF16 = jnp.bfloat16
VMEM = pl.BlockSpec(memory_space=pltpu.VMEM)
SMEM = pl.BlockSpec(memory_space=pltpu.SMEM)
PARAMS = pltpu.CompilerParams(vmem_limit_bytes=48 * 1024 * 1024)
EXTRA = 8


def exchange(x, axes):
    return lax.all_to_all(x, axes, 0, 0, tiled=True)


def copies(x, axes):
    count = lax.axis_size(axes)
    return exchange(jnp.broadcast_to(x[None], (count, *x.shape)), axes)


def along_z(x, step):
    n_zl, n_zh = lax.axis_size("zl"), lax.axis_size("zh")
    count = n_zl * n_zh
    at = [(z % n_zl) * n_zh + z // n_zl for z in range(count)]
    return lax.ppermute(x, ("zl", "zh"), [(at[z], at[(z + step) % count]) for z in range(count)])


def core_swap(x):
    return lax.ppermute(x, "co", [(0, 1), (1, 0)])


def block_of(z, core, n_zl, n_zh):
    return (z % n_zl) * (2 * n_zh) + core * n_zh + z // n_zl


def column(table, z, owner, n_zl, n_zh):
    first = block_of(z, 0, n_zl, n_zh)
    second = block_of(z, 1, n_zl, n_zh)
    return jnp.where(owner == 0, table[:, first : first + 1], table[:, second : second + 1])


def norm_kernel(n_zl, n_zh, at, mine, other, gain, shift, normed, stats):
    core = at[0]
    n_z, own_width, rows = mine.shape
    width = 2 * n_z * own_width

    def totals(i, carry):
        total, squares = carry
        for ref in (mine, other):
            x = ref[i].astype(F32)
            total = total + jnp.sum(x, 0, keepdims=True)
            squares = squares + jnp.sum(x * x, 0, keepdims=True)
        return total, squares

    zero = jnp.zeros((1, rows), F32)
    total, squares = lax.fori_loop(0, n_z, totals, (zero, zero))
    mean = total / width
    inv = lax.rsqrt(squares / width - mean * mean + EPSILON)
    stats[0:1, :] = mean
    stats[1:2, :] = inv
    for i in range(n_z):
        for ref, owner in ((mine, core), (other, 1 - core)):
            b = block_of(i, owner, n_zl, n_zh)
            scale = column(gain, i, owner, n_zl, n_zh)
            offset = column(shift, i, owner, n_zl, n_zh)
            value = (ref[i].astype(F32) - mean) * inv * scale + offset
            normed[b] = value.astype(BF16)


def high_low(plain, cross):
    high_plain, high_cross = plain.astype(BF16).astype(F32), cross.astype(BF16).astype(F32)
    pad = jnp.zeros((EXTRA - 4, plain.shape[1]), F32)
    return jnp.concatenate(
        [high_plain, plain - high_plain, high_cross, cross - high_cross, pad], 0
    ).astype(BF16)


def part_kernel(n_zl, n_zh, at, weight, d_embed, mine, other, gain, stats, keep, send):
    core = at[0]
    n_z, own_width, rows = mine.shape
    mean, inv = stats[0:1, :], stats[1:2, :]
    plain = cross = jnp.zeros((1, rows), F32)
    for i in range(n_z):
        for source, owner, out in ((mine, core, keep), (other, 1 - core, send)):
            b = block_of(i, owner, n_zl, n_zh)
            part = lax.dot_general(
                weight[b], d_embed[...], (((1,), (1,)), ((), ())), preferred_element_type=F32
            ).astype(BF16)
            out[i, 0:own_width, :] = part
            scaled = part.astype(F32) * column(gain, i, owner, n_zl, n_zh)
            xhat = (source[i].astype(F32) - mean) * inv
            plain = plain + jnp.sum(scaled, 0, keepdims=True)
            cross = cross + jnp.sum(scaled * xhat, 0, keepdims=True)
    tail = high_low(plain, cross)
    for i in range(n_z):
        keep[i, own_width:, :] = tail
        send[i, own_width:, :] = tail


def add_blocks(first, second):
    own_width = first.shape[0] - EXTRA
    a, b = first.astype(F32), second.astype(F32)
    tail = a[own_width:] + b[own_width:]
    return (a[:own_width] + b[:own_width]).astype(BF16), high_low(
        tail[0:1] + tail[1:2], tail[2:3] + tail[3:4]
    )


def pair_kernel(at, keep, recv, own, away):
    n_z, own_width = keep.shape[0], keep.shape[1] - EXTRA
    z = at[1]
    neighbour = z + 1 - 2 * lax.rem(z, 2)
    for out, start in ((own, z), (away, neighbour)):
        for j in range(n_z // 2):
            i = lax.rem(start + 2 * j, n_z)
            pair, tail = add_blocks(keep[i], recv[i])
            out[j, 0:own_width, :] = pair
            out[j, own_width:, :] = tail


def quad_kernel(own, recv, *outs):
    own_width = own.shape[1] - EXTRA
    for j, out in enumerate(outs):
        quad, tail = add_blocks(own[j], recv[j])
        out[0:own_width, :] = quad
        out[own_width:, :] = tail


def body(patches, gain, shift, proj_weight, llm_rank, embed_grad):
    rows, own_width = patches.shape
    width = gain.shape[0]
    out_cols = proj_weight.shape[1]
    n_y, n_x = lax.axis_size("y"), lax.axis_size("x")
    n_zl, n_zh = lax.axis_size("zl"), lax.axis_size("zh")
    n_z = n_zl * n_zh
    senders = n_y * n_x
    slice_rows = proj_weight.shape[0]
    padded_rows = (slice_rows + 2 + 7) // 8 * 8
    most = embed_grad.shape[0] // senders
    blocks = width // own_width
    core = lax.axis_index("co")
    at = jnp.stack([core, lax.axis_index(ZED)]).astype(jnp.int32)

    weight_x = copies(proj_weight, "x").reshape(n_x * slice_rows, out_cols)
    weight = lax.all_gather(weight_x, "y", axis=0, tiled=True)

    embed_grad, _ = lax.optimization_barrier((embed_grad, weight_x))
    returned = exchange(embed_grad.reshape(senders, most, out_cols), ENC)
    own_t = patches.T
    own_t, _ = lax.optimization_barrier((own_t, weight_x))
    mine = lax.all_gather(own_t, ZED, axis=0)
    other = core_swap(mine)

    gain_t, shift_t = gain.reshape(blocks, own_width).T, shift.reshape(blocks, own_width).T
    normed, stats = pl.pallas_call(
        functools.partial(norm_kernel, n_zl, n_zh),
        out_shape=(
            jax.ShapeDtypeStruct((blocks, own_width, rows), BF16),
            jax.ShapeDtypeStruct((8, rows), F32),
        ),
        in_specs=[SMEM] + [VMEM] * 4,
        out_specs=(VMEM,) * 2,
        compiler_params=PARAMS,
        name="norm",
    )(at, mine, other, gain_t, shift_t)
    mean, inv = stats[0], stats[1]
    normed = normed.reshape(width, rows)

    target = llm_rank[:, 0]
    owners = jnp.arange(senders, dtype=jnp.int32)
    hits = (target[:, None] == owners[None, :]).astype(jnp.int32)
    rank = jnp.sum((jnp.cumsum(hits, 0) - hits) * hits, 1)
    slot = target * most + rank
    d_embed = returned.reshape(senders * most, out_cols)[slot]

    grad_part = jnp.dot(normed, d_embed, preferred_element_type=F32).astype(BF16)
    grad_y = lax.psum_scatter(grad_part, "y", scatter_dimension=0, tiled=True)

    half_shape = jax.ShapeDtypeStruct((n_z, own_width + EXTRA, rows), BF16)
    keep, send = pl.pallas_call(
        functools.partial(part_kernel, n_zl, n_zh),
        out_shape=(half_shape, half_shape),
        in_specs=[SMEM] + [VMEM] * 6,
        out_specs=(VMEM,) * 2,
        compiler_params=PARAMS,
        name="part",
    )(
        at, weight.reshape(blocks, own_width, out_cols), d_embed, mine, other, gain_t, stats
    )
    recv = core_swap(send)

    weight_after, keep = lax.optimization_barrier((weight, keep))
    embed = lax.dot_general(
        normed, weight_after, (((0,), (0,)), ((), ())), preferred_element_type=F32
    ).astype(BF16)
    outgoing = jnp.zeros((senders * most, out_cols), BF16).at[slot].set(embed)

    pair_shape = jax.ShapeDtypeStruct((n_z // 2, own_width + EXTRA, rows), BF16)
    pair_own, pair_away = pl.pallas_call(
        pair_kernel,
        out_shape=(pair_shape, pair_shape),
        in_specs=[SMEM] + [VMEM] * 2,
        out_specs=(VMEM,) * 2,
        compiler_params=PARAMS,
        name="pair",
    )(at, keep, recv)
    pair_recv = lax.ppermute(pair_away, "zl", [(i, i ^ 1) for i in range(n_zl)])

    outgoing, _ = lax.optimization_barrier((outgoing, pair_away))
    embeds_recv = exchange(outgoing.reshape(senders, most, out_cols), ENC).reshape(
        senders * most, out_cols
    )

    quads = pl.pallas_call(
        quad_kernel,
        out_shape=(jax.ShapeDtypeStruct((own_width + EXTRA, rows), BF16),) * (n_z // 2),
        in_specs=[VMEM] * 2,
        out_specs=(VMEM,) * (n_z // 2),
        compiler_params=PARAMS,
        name="quad",
    )(pair_own, pair_recv)
    columns = sum(
        [along_z(quads[j], 2 * j).astype(F32) for j in range(1, n_z // 2)],
        quads[0].astype(F32),
    )
    dnormed = columns[:own_width]
    tail = columns[own_width:]
    plain = (tail[0] + tail[1]) / width
    cross = (tail[2] + tail[3]) / width

    column_start = lax.axis_index(COLS) * own_width
    gain_own = lax.dynamic_slice_in_dim(gain, column_start, own_width, 0)[:, None]
    xhat_own = (own_t.astype(F32) - mean) * inv
    hidden = (inv * (dnormed * gain_own - plain - xhat_own * cross)).astype(BF16).T
    sums = jnp.concatenate([jnp.sum(dnormed * xhat_own, 1), jnp.sum(dnormed, 1)])
    sums, embeds_recv = lax.optimization_barrier((sums, embeds_recv))
    sums = jnp.sum(copies(sums[None], "y"), (0, 1))

    high = lax.reduce_precision(sums, 8, 7)
    tail = jnp.stack([high, sums - high]).astype(BF16)
    tail = jnp.pad(tail, ((0, padded_rows - slice_rows - 2), (0, out_cols - sums.size)))
    grad_y, tail = lax.optimization_barrier((grad_y, tail))
    grad_x = jnp.concatenate(
        [
            grad_y.reshape(n_x, slice_rows, out_cols),
            jnp.broadcast_to(tail[None], (n_x, *tail.shape)),
        ],
        1,
    )
    total = jnp.sum(exchange(grad_x, "x").astype(F32), 0)
    grad_weight = total[:slice_rows]
    sums = total[slice_rows] + total[slice_rows + 1]
    return (
        embeds_recv,
        hidden,
        grad_weight,
        sums[:own_width],
        sums[own_width : 2 * own_width],
    )


def solution(mesh):
    devices = mesh.devices
    split = Mesh(devices.reshape(8, 4, 4, 2, 2), ("y", "x", "zl", "co", "zh"))
    spec = P(ENC, COLS)
    in_specs = (spec, P(), P(), spec, P(ENC, None), spec)
    out_specs = (spec, spec, spec, P(COLS), P(COLS))
    return jax.shard_map(body, mesh=split, in_specs=in_specs, out_specs=out_specs, check_vma=False)
```

```python
import functools

import jax
import jax.numpy as jnp
from jax import lax
from jax.experimental import pallas as pl
from jax.experimental.pallas import tpu as pltpu
from jax.sharding import Mesh
from jax.sharding import PartitionSpec as P

ENC = ("y", "x")
COLS = ("zl", "co", "zh")
ZED = ("zh", "zl")
EPSILON = 1e-05
F32 = jnp.float32
BF16 = jnp.bfloat16
VMEM = pl.BlockSpec(memory_space=pltpu.VMEM)
SMEM = pl.BlockSpec(memory_space=pltpu.SMEM)
PARAMS = pltpu.CompilerParams(vmem_limit_bytes=48 * 1024 * 1024)
EXTRA = 8


def exchange(x, axes):
    return lax.all_to_all(x, axes, 0, 0, tiled=True)


def copies(x, axes):
    count = lax.axis_size(axes)
    return exchange(jnp.broadcast_to(x[None], (count, *x.shape)), axes)


def along_z(x, step):
    n_zl, n_zh = lax.axis_size("zl"), lax.axis_size("zh")
    count = n_zl * n_zh
    at = [(z % n_zl) * n_zh + z // n_zl for z in range(count)]
    return lax.ppermute(x, ("zl", "zh"), [(at[z], at[(z + step) % count]) for z in range(count)])


def core_swap(x):
    return lax.ppermute(x, "co", [(0, 1), (1, 0)])


def block_of(z, core, n_zl, n_zh):
    return (z % n_zl) * (2 * n_zh) + core * n_zh + z // n_zl


def column(table, z, owner, n_zl, n_zh):
    first = block_of(z, 0, n_zl, n_zh)
    second = block_of(z, 1, n_zl, n_zh)
    return jnp.where(owner == 0, table[:, first : first + 1], table[:, second : second + 1])


def norm_kernel(n_zl, n_zh, at, mine, other, gain, shift, normed, stats):
    core = at[0]
    n_z, own_width, rows = mine.shape
    width = 2 * n_z * own_width

    def totals(i, carry):
        total, squares = carry
        for ref in (mine, other):
            x = ref[i].astype(F32)
            total = total + jnp.sum(x, 0, keepdims=True)
            squares = squares + jnp.sum(x * x, 0, keepdims=True)
        return total, squares

    zero = jnp.zeros((1, rows), F32)
    total, squares = lax.fori_loop(0, n_z, totals, (zero, zero))
    mean = total / width
    inv = lax.rsqrt(squares / width - mean * mean + EPSILON)
    stats[0:1, :] = mean
    stats[1:2, :] = inv
    for i in range(n_z):
        for ref, owner in ((mine, core), (other, 1 - core)):
            b = block_of(i, owner, n_zl, n_zh)
            scale = column(gain, i, owner, n_zl, n_zh)
            offset = column(shift, i, owner, n_zl, n_zh)
            value = (ref[i].astype(F32) - mean) * inv * scale + offset
            normed[b] = value.astype(BF16)


def high_low(plain, cross):
    high_plain, high_cross = plain.astype(BF16).astype(F32), cross.astype(BF16).astype(F32)
    pad = jnp.zeros((EXTRA - 4, plain.shape[1]), F32)
    return jnp.concatenate(
        [high_plain, plain - high_plain, high_cross, cross - high_cross, pad], 0
    ).astype(BF16)


def part_kernel(n_zl, n_zh, at, weight, d_embed, mine, other, gain, stats, keep, send):
    core = at[0]
    n_z, own_width, rows = mine.shape
    mean, inv = stats[0:1, :], stats[1:2, :]
    plain = cross = jnp.zeros((1, rows), F32)
    for i in range(n_z):
        for source, owner, out in ((mine, core, keep), (other, 1 - core, send)):
            b = block_of(i, owner, n_zl, n_zh)
            part = lax.dot_general(
                weight[b], d_embed[...], (((1,), (1,)), ((), ())), preferred_element_type=F32
            ).astype(BF16)
            out[i, 0:own_width, :] = part
            scaled = part.astype(F32) * column(gain, i, owner, n_zl, n_zh)
            xhat = (source[i].astype(F32) - mean) * inv
            plain = plain + jnp.sum(scaled, 0, keepdims=True)
            cross = cross + jnp.sum(scaled * xhat, 0, keepdims=True)
    tail = high_low(plain, cross)
    for i in range(n_z):
        keep[i, own_width:, :] = tail
        send[i, own_width:, :] = tail


def add_blocks(first, second):
    own_width = first.shape[0] - EXTRA
    a, b = first.astype(F32), second.astype(F32)
    tail = a[own_width:] + b[own_width:]
    return (a[:own_width] + b[:own_width]).astype(BF16), high_low(
        tail[0:1] + tail[1:2], tail[2:3] + tail[3:4]
    )


def pair_kernel(at, keep, recv, own, away):
    n_z, own_width = keep.shape[0], keep.shape[1] - EXTRA
    z = at[1]
    neighbour = z + 1 - 2 * lax.rem(z, 2)
    for out, start in ((own, z), (away, neighbour)):
        for j in range(n_z // 2):
            i = lax.rem(start + 2 * j, n_z)
            pair, tail = add_blocks(keep[i], recv[i])
            out[j, 0:own_width, :] = pair
            out[j, own_width:, :] = tail


def quad_kernel(own, recv, *outs):
    own_width = own.shape[1] - EXTRA
    for j, out in enumerate(outs):
        quad, tail = add_blocks(own[j], recv[j])
        out[0:own_width, :] = quad
        out[own_width:, :] = tail


def body(patches, gain, shift, proj_weight, llm_rank, embed_grad):
    rows, own_width = patches.shape
    width = gain.shape[0]
    out_cols = proj_weight.shape[1]
    n_y, n_x = lax.axis_size("y"), lax.axis_size("x")
    n_zl, n_zh = lax.axis_size("zl"), lax.axis_size("zh")
    n_z = n_zl * n_zh
    senders = n_y * n_x
    slice_rows = proj_weight.shape[0]
    padded_rows = (slice_rows + 2 + 7) // 8 * 8
    most = embed_grad.shape[0] // senders
    blocks = width // own_width
    core = lax.axis_index("co")
    at = jnp.stack([core, lax.axis_index(ZED)]).astype(jnp.int32)

    weight_x = copies(proj_weight, "x").reshape(n_x * slice_rows, out_cols)
    weight = lax.all_gather(weight_x, "y", axis=0, tiled=True)

    embed_grad, _ = lax.optimization_barrier((embed_grad, weight_x))
    returned = exchange(embed_grad.reshape(senders, most, out_cols), ENC)
    own_t = patches.T
    own_t, _ = lax.optimization_barrier((own_t, weight_x))
    mine = lax.all_gather(own_t, ZED, axis=0)
    other = core_swap(mine)

    gain_t, shift_t = gain.reshape(blocks, own_width).T, shift.reshape(blocks, own_width).T
    normed, stats = pl.pallas_call(
        functools.partial(norm_kernel, n_zl, n_zh),
        out_shape=(
            jax.ShapeDtypeStruct((blocks, own_width, rows), BF16),
            jax.ShapeDtypeStruct((8, rows), F32),
        ),
        in_specs=[SMEM] + [VMEM] * 4,
        out_specs=(VMEM,) * 2,
        compiler_params=PARAMS,
        name="norm",
    )(at, mine, other, gain_t, shift_t)
    mean, inv = stats[0], stats[1]
    normed = normed.reshape(width, rows)

    target = llm_rank[:, 0]
    owners = jnp.arange(senders, dtype=jnp.int32)
    hits = (target[:, None] == owners[None, :]).astype(jnp.int32)
    rank = jnp.sum((jnp.cumsum(hits, 0) - hits) * hits, 1)
    slot = target * most + rank
    d_embed = returned.reshape(senders * most, out_cols)[slot]

    grad_part = jnp.dot(normed, d_embed, preferred_element_type=F32).astype(BF16)
    grad_y = lax.psum_scatter(grad_part, "y", scatter_dimension=0, tiled=True)

    embed = lax.dot_general(
        normed, weight, (((0,), (0,)), ((), ())), preferred_element_type=F32
    ).astype(BF16)
    outgoing = jnp.zeros((senders * most, out_cols), BF16).at[slot].set(embed)
    embeds_recv = exchange(outgoing.reshape(senders, most, out_cols), ENC).reshape(
        senders * most, out_cols
    )
    weight, _ = lax.optimization_barrier((weight, outgoing))

    half_shape = jax.ShapeDtypeStruct((n_z, own_width + EXTRA, rows), BF16)
    keep, send = pl.pallas_call(
        functools.partial(part_kernel, n_zl, n_zh),
        out_shape=(half_shape, half_shape),
        in_specs=[SMEM] + [VMEM] * 6,
        out_specs=(VMEM,) * 2,
        compiler_params=PARAMS,
        name="part",
    )(
        at, weight.reshape(blocks, own_width, out_cols), d_embed, mine, other, gain_t, stats
    )
    recv = core_swap(send)


    pair_shape = jax.ShapeDtypeStruct((n_z // 2, own_width + EXTRA, rows), BF16)
    pair_own, pair_away = pl.pallas_call(
        pair_kernel,
        out_shape=(pair_shape, pair_shape),
        in_specs=[SMEM] + [VMEM] * 2,
        out_specs=(VMEM,) * 2,
        compiler_params=PARAMS,
        name="pair",
    )(at, keep, recv)
    pair_recv = lax.ppermute(pair_away, "zl", [(i, i ^ 1) for i in range(n_zl)])


    quads = pl.pallas_call(
        quad_kernel,
        out_shape=(jax.ShapeDtypeStruct((own_width + EXTRA, rows), BF16),) * (n_z // 2),
        in_specs=[VMEM] * 2,
        out_specs=(VMEM,) * (n_z // 2),
        compiler_params=PARAMS,
        name="quad",
    )(pair_own, pair_recv)
    columns = sum(
        [along_z(quads[j], 2 * j).astype(F32) for j in range(1, n_z // 2)],
        quads[0].astype(F32),
    )
    dnormed = columns[:own_width]
    tail = columns[own_width:]
    plain = (tail[0] + tail[1]) / width
    cross = (tail[2] + tail[3]) / width

    column_start = lax.axis_index(COLS) * own_width
    gain_own = lax.dynamic_slice_in_dim(gain, column_start, own_width, 0)[:, None]
    xhat_own = (own_t.astype(F32) - mean) * inv
    hidden = (inv * (dnormed * gain_own - plain - xhat_own * cross)).astype(BF16).T
    sums = jnp.concatenate([jnp.sum(dnormed * xhat_own, 1), jnp.sum(dnormed, 1)])
    sums, embeds_recv = lax.optimization_barrier((sums, embeds_recv))
    sums = jnp.sum(copies(sums[None], "y"), (0, 1))

    high = lax.reduce_precision(sums, 8, 7)
    tail = jnp.stack([high, sums - high]).astype(BF16)
    tail = jnp.pad(tail, ((0, padded_rows - slice_rows - 2), (0, out_cols - sums.size)))
    grad_y, tail = lax.optimization_barrier((grad_y, tail))
    grad_x = jnp.concatenate(
        [
            grad_y.reshape(n_x, slice_rows, out_cols),
            jnp.broadcast_to(tail[None], (n_x, *tail.shape)),
        ],
        1,
    )
    total = jnp.sum(exchange(grad_x, "x").astype(F32), 0)
    grad_weight = total[:slice_rows]
    sums = total[slice_rows] + total[slice_rows + 1]
    return (
        embeds_recv,
        hidden,
        grad_weight,
        sums[:own_width],
        sums[own_width : 2 * own_width],
    )


def solution(mesh):
    devices = mesh.devices
    split = Mesh(devices.reshape(8, 4, 4, 2, 2), ("y", "x", "zl", "co", "zh"))
    spec = P(ENC, COLS)
    in_specs = (spec, P(), P(), spec, P(ENC, None), spec)
    out_specs = (spec, spec, spec, P(COLS), P(COLS))
    return jax.shard_map(body, mesh=split, in_specs=in_specs, out_specs=out_specs, check_vma=False)
```

```python
import functools

import jax
import jax.numpy as jnp
from jax import lax
from jax.experimental import pallas as pl
from jax.experimental.pallas import tpu as pltpu
from jax.sharding import Mesh
from jax.sharding import PartitionSpec as P

ENC = ("y", "x")
COLS = ("zl", "co", "zh")
ZED = ("zh", "zl")
EPSILON = 1e-05
F32 = jnp.float32
BF16 = jnp.bfloat16
VMEM = pl.BlockSpec(memory_space=pltpu.VMEM)
SMEM = pl.BlockSpec(memory_space=pltpu.SMEM)
PARAMS = pltpu.CompilerParams(vmem_limit_bytes=48 * 1024 * 1024)
EXTRA = 8


def exchange(x, axes):
    return lax.all_to_all(x, axes, 0, 0, tiled=True)


def copies(x, axes):
    count = lax.axis_size(axes)
    return exchange(jnp.broadcast_to(x[None], (count, *x.shape)), axes)


def along_z(x, step):
    n_zl, n_zh = lax.axis_size("zl"), lax.axis_size("zh")
    count = n_zl * n_zh
    at = [(z % n_zl) * n_zh + z // n_zl for z in range(count)]
    return lax.ppermute(x, ("zl", "zh"), [(at[z], at[(z + step) % count]) for z in range(count)])


def core_swap(x):
    return lax.ppermute(x, "co", [(0, 1), (1, 0)])


def block_of(z, core, n_zl, n_zh):
    return (z % n_zl) * (2 * n_zh) + core * n_zh + z // n_zl


def column(table, z, owner, n_zl, n_zh):
    first = block_of(z, 0, n_zl, n_zh)
    second = block_of(z, 1, n_zl, n_zh)
    return jnp.where(owner == 0, table[:, first : first + 1], table[:, second : second + 1])


def norm_kernel(n_zl, n_zh, at, mine, other, gain, shift, normed, stats):
    core = at[0]
    n_z, own_width, rows = mine.shape
    width = 2 * n_z * own_width

    def totals(i, carry):
        total, squares = carry
        for ref in (mine, other):
            x = ref[i].astype(F32)
            total = total + jnp.sum(x, 0, keepdims=True)
            squares = squares + jnp.sum(x * x, 0, keepdims=True)
        return total, squares

    zero = jnp.zeros((1, rows), F32)
    total, squares = lax.fori_loop(0, n_z, totals, (zero, zero))
    mean = total / width
    inv = lax.rsqrt(squares / width - mean * mean + EPSILON)
    stats[0:1, :] = mean
    stats[1:2, :] = inv
    for i in range(n_z):
        for ref, owner in ((mine, core), (other, 1 - core)):
            b = block_of(i, owner, n_zl, n_zh)
            scale = column(gain, i, owner, n_zl, n_zh)
            offset = column(shift, i, owner, n_zl, n_zh)
            value = (ref[i].astype(F32) - mean) * inv * scale + offset
            normed[b] = value.astype(BF16)


def high_low(plain, cross):
    high_plain, high_cross = plain.astype(BF16).astype(F32), cross.astype(BF16).astype(F32)
    pad = jnp.zeros((EXTRA - 4, plain.shape[1]), F32)
    return jnp.concatenate(
        [high_plain, plain - high_plain, high_cross, cross - high_cross, pad], 0
    ).astype(BF16)


def part_kernel(n_zl, n_zh, at, weight, d_embed, mine, other, gain, stats, keep, send):
    core = at[0]
    n_z, own_width, rows = mine.shape
    mean, inv = stats[0:1, :], stats[1:2, :]
    plain = cross = jnp.zeros((1, rows), F32)
    for i in range(n_z):
        for source, owner, out in ((mine, core, keep), (other, 1 - core, send)):
            b = block_of(i, owner, n_zl, n_zh)
            part = lax.dot_general(
                weight[b], d_embed[...], (((1,), (1,)), ((), ())), preferred_element_type=F32
            ).astype(BF16)
            out[i, 0:own_width, :] = part
            scaled = part.astype(F32) * column(gain, i, owner, n_zl, n_zh)
            xhat = (source[i].astype(F32) - mean) * inv
            plain = plain + jnp.sum(scaled, 0, keepdims=True)
            cross = cross + jnp.sum(scaled * xhat, 0, keepdims=True)
    tail = high_low(plain, cross)
    for i in range(n_z):
        keep[i, own_width:, :] = tail
        send[i, own_width:, :] = tail


def add_blocks(first, second):
    own_width = first.shape[0] - EXTRA
    a, b = first.astype(F32), second.astype(F32)
    tail = a[own_width:] + b[own_width:]
    return (a[:own_width] + b[:own_width]).astype(BF16), high_low(
        tail[0:1] + tail[1:2], tail[2:3] + tail[3:4]
    )


def pair_kernel(at, keep, recv, own, away):
    n_z, own_width = keep.shape[0], keep.shape[1] - EXTRA
    z = at[1]
    neighbour = z + 1 - 2 * lax.rem(z, 2)
    for out, start in ((own, z), (away, neighbour)):
        for j in range(n_z // 2):
            i = lax.rem(start + 2 * j, n_z)
            pair, tail = add_blocks(keep[i], recv[i])
            out[j, 0:own_width, :] = pair
            out[j, own_width:, :] = tail


def quad_kernel(own, recv, *outs):
    own_width = own.shape[1] - EXTRA
    for j, out in enumerate(outs):
        quad, tail = add_blocks(own[j], recv[j])
        out[0:own_width, :] = quad
        out[own_width:, :] = tail


def body(patches, gain, shift, proj_weight, llm_rank, embed_grad):
    rows, own_width = patches.shape
    width = gain.shape[0]
    out_cols = proj_weight.shape[1]
    n_y, n_x = lax.axis_size("y"), lax.axis_size("x")
    n_zl, n_zh = lax.axis_size("zl"), lax.axis_size("zh")
    n_z = n_zl * n_zh
    senders = n_y * n_x
    slice_rows = proj_weight.shape[0]
    padded_rows = (slice_rows + 2 + 7) // 8 * 8
    most = embed_grad.shape[0] // senders
    blocks = width // own_width
    core = lax.axis_index("co")
    at = jnp.stack([core, lax.axis_index(ZED)]).astype(jnp.int32)

    weight_x = copies(proj_weight, "x").reshape(n_x * slice_rows, out_cols)
    weight = lax.all_gather(weight_x, "y", axis=0, tiled=True)

    embed_grad, _ = lax.optimization_barrier((embed_grad, weight_x))
    returned = exchange(embed_grad.reshape(senders, most, out_cols), ENC)
    own_t = patches.T
    own_t, _ = lax.optimization_barrier((own_t, weight_x))
    mine = lax.all_gather(own_t, ZED, axis=0)
    other = core_swap(mine)

    gain_t, shift_t = gain.reshape(blocks, own_width).T, shift.reshape(blocks, own_width).T
    normed, stats = pl.pallas_call(
        functools.partial(norm_kernel, n_zl, n_zh),
        out_shape=(
            jax.ShapeDtypeStruct((blocks, own_width, rows), BF16),
            jax.ShapeDtypeStruct((8, rows), F32),
        ),
        in_specs=[SMEM] + [VMEM] * 4,
        out_specs=(VMEM,) * 2,
        compiler_params=PARAMS,
        name="norm",
    )(at, mine, other, gain_t, shift_t)
    mean, inv = stats[0], stats[1]
    normed = normed.reshape(width, rows)

    target = llm_rank[:, 0]
    owners = jnp.arange(senders, dtype=jnp.int32)
    hits = (target[:, None] == owners[None, :]).astype(jnp.int32)
    rank = jnp.sum((jnp.cumsum(hits, 0) - hits) * hits, 1)
    slot = target * most + rank
    d_embed = returned.reshape(senders * most, out_cols)[slot]

    grad_part = jnp.dot(normed, d_embed, preferred_element_type=F32).astype(BF16)
    grad_y = lax.psum_scatter(grad_part, "y", scatter_dimension=0, tiled=True)

    half_shape = jax.ShapeDtypeStruct((n_z, own_width + EXTRA, rows), BF16)
    keep, send = pl.pallas_call(
        functools.partial(part_kernel, n_zl, n_zh),
        out_shape=(half_shape, half_shape),
        in_specs=[SMEM] + [VMEM] * 6,
        out_specs=(VMEM,) * 2,
        compiler_params=PARAMS,
        name="part",
    )(
        at, weight.reshape(blocks, own_width, out_cols), d_embed, mine, other, gain_t, stats
    )
    recv = core_swap(send)

    weight_after, keep = lax.optimization_barrier((weight, keep))
    embed = lax.dot_general(
        normed, weight_after, (((0,), (0,)), ((), ())), preferred_element_type=F32
    ).astype(BF16)
    outgoing = jnp.zeros((senders * most, out_cols), BF16).at[slot].set(embed)

    pair_shape = jax.ShapeDtypeStruct((n_z // 2, own_width + EXTRA, rows), BF16)
    pair_own, pair_away = pl.pallas_call(
        pair_kernel,
        out_shape=(pair_shape, pair_shape),
        in_specs=[SMEM] + [VMEM] * 2,
        out_specs=(VMEM,) * 2,
        compiler_params=PARAMS,
        name="pair",
    )(at, keep, recv)
    pair_recv = lax.ppermute(pair_away, "zl", [(i, i ^ 1) for i in range(n_zl)])

    outgoing, _ = lax.optimization_barrier((outgoing, pair_away))
    embeds_recv = exchange(outgoing.reshape(senders, most, out_cols), ENC).reshape(
        senders * most, out_cols
    )

    quads = pl.pallas_call(
        quad_kernel,
        out_shape=(jax.ShapeDtypeStruct((own_width + EXTRA, rows), BF16),) * (n_z // 2),
        in_specs=[VMEM] * 2,
        out_specs=(VMEM,) * (n_z // 2),
        compiler_params=PARAMS,
        name="quad",
    )(pair_own, pair_recv)
    columns = sum(
        [along_z(quads[j], 2 * j).astype(F32) for j in range(1, n_z // 2)],
        quads[0].astype(F32),
    )
    dnormed = columns[:own_width]
    tail = columns[own_width:]
    plain = (tail[0] + tail[1]) / width
    cross = (tail[2] + tail[3]) / width

    column_start = lax.axis_index(COLS) * own_width
    gain_own = lax.dynamic_slice_in_dim(gain, column_start, own_width, 0)[:, None]
    xhat_own = (own_t.astype(F32) - mean) * inv
    hidden = (inv * (dnormed * gain_own - plain - xhat_own * cross)).astype(BF16).T
    sums = jnp.concatenate([jnp.sum(dnormed * xhat_own, 1), jnp.sum(dnormed, 1)])
    grad_y, _ = lax.optimization_barrier((grad_y, sums))
    sums, embeds_recv = lax.optimization_barrier((sums, embeds_recv))
    sums = jnp.sum(copies(sums[None], "y"), (0, 1))

    high = lax.reduce_precision(sums, 8, 7)
    tail = jnp.stack([high, sums - high]).astype(BF16)
    tail = jnp.pad(tail, ((0, padded_rows - slice_rows - 2), (0, out_cols - sums.size)))
    grad_y, tail = lax.optimization_barrier((grad_y.reshape(n_x, slice_rows, out_cols), tail))
    grad_x = jnp.concatenate(
        [
            grad_y,
            jnp.broadcast_to(tail[None], (n_x, *tail.shape)),
        ],
        1,
    )
    total = jnp.sum(exchange(grad_x, "x").astype(F32), 0)
    grad_weight = total[:slice_rows]
    sums = total[slice_rows] + total[slice_rows + 1]
    return (
        embeds_recv,
        hidden,
        grad_weight,
        sums[:own_width],
        sums[own_width : 2 * own_width],
    )


def solution(mesh):
    devices = mesh.devices
    split = Mesh(devices.reshape(8, 4, 4, 2, 2), ("y", "x", "zl", "co", "zh"))
    spec = P(ENC, COLS)
    in_specs = (spec, P(), P(), spec, P(ENC, None), spec)
    out_specs = (spec, spec, spec, P(COLS), P(COLS))
    return jax.shard_map(body, mesh=split, in_specs=in_specs, out_specs=out_specs, check_vma=False)
```
